32 devices in a mesh: dp: 16 (over z, y, core), tensor: 2 (over x).
Axes of the slice: x: 2, y: 2, z: 4, core: 2. Of those that a mesh axis runs over, the one named last changes fastest.
Arguments:
- inputs: bfloat16 [16384, 1536], P(('dp', 'tensor')), may hold values from -6 to 6
- gain_attn: bfloat16 [1536], P('dp'), may hold values from 0.5 to 1.5
- w_query: bfloat16 [1536, 1536], P('dp', 'tensor'), may hold values from -0.21875 to 0.21875
- w_key: bfloat16 [1536, 512], P('dp', 'tensor'), may hold values from -0.15625 to 0.15625
- w_value: bfloat16 [1536, 512], P('dp', 'tensor'), may hold values from -0.15625 to 0.15625
- w_out: bfloat16 [1536, 1536], P('tensor', 'dp'), may hold values from -1.25 to 1.25
- gain_moe: bfloat16 [1536], P('dp'), may hold values from 0.5 to 1.5
- w_router: bfloat16 [1536, 40], P('dp'), may hold values from -0.078125 to 0.078125
- w_gate: bfloat16 [40, 786432], P(None, ('dp', 'tensor')), may hold values from -0.15625 to 0.15625
- w_up: bfloat16 [40, 786432], P(None, ('dp', 'tensor')), may hold values from -0.15625 to 0.15625
- w_down: bfloat16 [40, 786432], P(None, ('dp', 'tensor')), may hold values from -0.5 to 0.5
- routes: int32 [16384, 8], P('dp'), may hold values from 0 to 39, all different within a row; in each aligned block of 1024 rows (0 to 1023, 1024 to 2047, ...) at most 256 rows name the same one
- cotangent: bfloat16 [16384, 1536], P(('dp', 'tensor')), may hold values from -6 to 6
Outputs:
- outputs: bfloat16 [16384, 1536], P(('dp', 'tensor'))
- input_grad: float32 [16384, 1536], P(('dp', 'tensor'))
- gain_attn_grad: float32 [1536], P('dp')
- w_query_grad: float32 [1536, 1536], P('dp', 'tensor')
- w_key_grad: float32 [1536, 512], P('dp', 'tensor')
- w_value_grad: float32 [1536, 512], P('dp', 'tensor')
- w_out_grad: float32 [1536, 1536], P('tensor', 'dp')
- gain_moe_grad: float32 [1536], P('dp')
- w_router_grad: float32 [1536, 40], P('dp')
- w_gate_grad: float32 [40, 786432], P(None, ('dp', 'tensor'))
- w_up_grad: float32 [40, 786432], P(None, ('dp', 'tensor'))
- w_down_grad: float32 [40, 786432], P(None, ('dp', 'tensor'))
The draws below stay inside these ranges and needn't reach their ends.
Inputs may be any that keep to these rules, and one draw needn't show every extreme that they name: `routes`: each row names 8 different experts. Within one sequence's 1024 rows no expert is named by more than 256 rows, and in some sequence one expert is named by exactly 256 rows.
All inputs are finite; a program needn't handle non-finite values.
Results may differ from the reference program's by a relative error of at most 0.025.
Values may be sent and summed in bfloat16 or wider, within the bound.
A program may use at most 512 MiB of HBM per device.

```python
import math
import jax
import jax.numpy as jnp
import numpy as np
from jax import lax

D = 1536
H = 24
KV = 8
HD = 64
E = 40
FF = 512
TOP = 8
SEQ = 1024
CAP = 256
TOKENS = 16384
N_DP = 16


def level_of(own_key, dims, pieces, smallest, high):
    loudness = 1.0
    for dim, parts in pieces:
        steps = jax.random.uniform(jax.random.fold_in(jax.random.fold_in(own_key, 6), dim), (parts,), jnp.float32, smallest / len(pieces), high / len(pieces))
        loudness = loudness * jnp.repeat(jnp.exp(steps), dims[dim] // parts).reshape((-1,) + (1,) * (len(dims) - 1 - dim))
    return loudness


def assign_block(rng, own, number, rows, number_of, top, most, slope):
    ranking = jax.random.permutation(rng, number_of)
    crowded, ordinary = shares(number_of, rows * top, most, slope, True), shares(number_of, rows * top, most, slope, False)
    places = jnp.arange(number_of)

    def named(sizes, offset_by):
        used = int((sizes > 0).sum())
        fixed = max(1, used // 4)
        moved = fixed + (places - fixed + offset_by * (used - fixed)) % max(1, number_of - fixed)
        return jnp.zeros((number_of,), jnp.int32).at[ranking[jnp.where(places < fixed, places, moved)]].set(jnp.asarray(sizes, jnp.int32))

    sizes = jnp.where(number % 4 == 0, named(crowded, number // 4), named(ordinary, number - number // 4 - 1))
    mixed = jax.random.permutation(jax.random.fold_in(own, 3), number_of)
    source_of, taker = mixed[0:number_of // 2 * 2:2], mixed[1:number_of // 2 * 2:2]
    margin = jnp.minimum(sizes[source_of] - 1, most - sizes[taker]) // 2
    margin = jnp.where((source_of == ranking[0]) | (taker == ranking[0]) | (sizes[taker] == 0), 0, jnp.maximum(margin, 0))
    moved = jax.random.randint(jax.random.fold_in(own, 4), (number_of // 2,), 0, 1 << 20) % (margin + 1)
    sizes = sizes.at[source_of].add(-moved).at[taker].add(moved)
    members = jnp.searchsorted(jnp.cumsum(sizes), jnp.arange(rows * top), side="right").astype(jnp.int32)
    table = members.reshape(top, rows).T
    table = table[jax.random.permutation(jax.random.fold_in(own, 1), rows)]
    offset_by = jax.random.randint(jax.random.fold_in(own, 2), (rows, 1), 0, top)
    return jnp.take_along_axis(table, (jnp.arange(top)[None, :] + offset_by) % top, axis=1)


def shares(number_of, total, reach, lean, full):
    portions = [(1 << 20) // math.isqrt(rank ** lean) + 1 for rank in range(1, number_of + 1)]
    largest = reach if full else min(reach, max(-(-total // number_of), total * portions[0] // sum(portions)))
    least = 1 if total - largest >= number_of - 1 else 0
    given, spare = [largest] + [least] * (number_of - 1), total - largest - least * (number_of - 1)
    while spare > 0:
        candidates = [i for i in range(1, number_of) if given[i] < largest] or [i for i in range(1, number_of) if given[i] < reach]
        mass, remaining = sum([portions[i] for i in candidates]), spare
        for i in candidates:
            more = min(reach - given[i], max(1, remaining * portions[i] // mass), spare)
            given[i] = given[i] + more
            spare = spare - more
    return np.array(given)


def centred(key, shape, scale, most, cuts=(), kind=jnp.bfloat16):
    factor_of = level_of(key, shape, cuts, -0.22, 0.18) if cuts else 1.0
    entries = jax.random.normal(key, shape, jnp.float32) * scale * factor_of
    return jnp.minimum(jnp.maximum(entries, -most), most).astype(kind)


def setup_inputs(seed: int = 0) -> dict:
    splits = jax.random.split(jax.random.key(seed), 14)
    inputs = centred(splits[0], (TOKENS, D), 1.0, 6.0, ((0, 32),))
    gain_attn = jnp.clip(1.0 + 0.1 * jax.random.normal(splits[1], (D,), jnp.float32), 0.5, 1.5).astype(jnp.bfloat16)
    w_query = centred(splits[2], (D, H * HD), (D // 2) ** -0.5, 0.21875, ((0, 16), (1, 2)))
    w_key = centred(splits[3], (D, KV * HD), D ** -0.5, 0.15625, ((0, 16), (1, 2)))
    w_value = centred(splits[4], (D, KV * HD), D ** -0.5, 0.15625, ((0, 16), (1, 2)))
    w_out = centred(splits[5], (H * HD, D), (H * HD // 64) ** -0.5, 1.25, ((0, 2), (1, 16)))
    gain_moe = jnp.clip(1.0 + 0.1 * jax.random.normal(splits[6], (D,), jnp.float32), 0.5, 1.5).astype(jnp.bfloat16)
    w_router = centred(splits[7], (D, E), (4 * D) ** -0.5, 0.078125, ((0, 16),))
    w_gate = centred(splits[8], (E, FF * D), D ** -0.5, 0.15625, ((1, 32),))
    w_up = centred(splits[9], (E, FF * D), D ** -0.5, 0.15625, ((1, 32),))
    w_down = centred(splits[10], (E, FF * D), (FF // 4) ** -0.5, 0.5, ((1, 32),))
    routes_keys = jax.random.split(jax.random.fold_in(splits[11], 1), TOKENS // SEQ)
    routes_turns = jax.random.permutation(jax.random.fold_in(splits[11], 3), TOKENS // SEQ)
    routes = jax.vmap(lambda own, number: assign_block(jax.random.fold_in(splits[11], 2), own, number, SEQ, E, TOP, CAP, 0))(routes_keys, routes_turns).reshape((TOKENS, TOP))
    cotangent = centred(splits[12], (TOKENS, D), 1.0, 6.0, ((0, 32),))
    return dict(inputs=inputs, gain_attn=gain_attn, w_query=w_query, w_key=w_key, w_value=w_value, w_out=w_out, gain_moe=gain_moe, w_router=w_router, w_gate=w_gate, w_up=w_up, w_down=w_down, routes=routes, cotangent=cotangent)


@jax.custom_vjp
def low(v):
    return lax.optimization_barrier(v.astype(jnp.bfloat16)).astype(jnp.float32)

@jax.custom_vjp
def low_back(v):
    return v

def low_keep(v):
    return (low(v), None)

def low_pass(kept, grad):
    return (grad,)

def back_keep(v):
    return (v, None)

def back_low(kept, grad):
    return (low(grad),)
low.defvjp(low_keep, low_pass)
low_back.defvjp(back_keep, back_low)
epsilon = 1e-06
highest = lax.Precision.HIGHEST

def matmul(left, right):
    return jnp.dot(left, right, precision=highest)

def rope_tables(seq_len, width):
    position = jnp.arange(seq_len).astype(jnp.float32)
    freq = 10000.0 ** (-jnp.arange(width // 2).astype(jnp.float32) * 2.0 / width)
    angle = position[:, None] * freq[None, :]
    return (jnp.cos(angle)[:, None, :], jnp.sin(angle)[:, None, :])

def rotate(values, cosine, sine):
    half = values.shape[-1] // 2
    first_half = values[..., :half]
    second_half = values[..., half:]
    return jnp.concatenate([first_half * cosine - second_half * sine, second_half * cosine + first_half * sine], axis=-1)

def rms_scale(values):
    return values * lax.rsqrt(lax.optimization_barrier(jnp.mean(values * values, axis=-1, keepdims=True)) + epsilon)

def slot_table(routes_seq):
    flat_ids = routes_seq.reshape(-1)
    onehot = (flat_ids[:, None] == jnp.arange(E, dtype=jnp.int32)[None, :]).astype(jnp.int32)
    before = jnp.cumsum(onehot, axis=0) - onehot
    return (flat_ids * CAP + lax.optimization_barrier(jnp.sum(before * onehot, axis=1))).astype(jnp.int32)

def attend(query_rot, key_rot, value_hd):
    seq_len = query_rot.shape[0]
    block_rows = min(512, seq_len)
    num_blocks = seq_len // block_rows
    grouped = query_rot.reshape(num_blocks, block_rows, KV, H // KV, HD)
    key_pos = jnp.arange(seq_len, dtype=jnp.int32)

    def one_block(block_item):
        query_blk, offset = block_item
        scores = jnp.einsum('qcgd,kcd->cgqk', query_blk, key_rot, precision=highest) * HD ** (-0.5)
        scores = low_back(scores)
        causal = (offset + jnp.arange(block_rows, dtype=jnp.int32))[:, None] >= key_pos[None, :]
        scores = jnp.where(causal, scores, -1e+30)
        attn_prob = low(jax.nn.softmax(scores, axis=-1))
        return jnp.einsum('cgqk,kcd->qcgd', attn_prob, value_hd, precision=highest)
    offsets = jnp.arange(num_blocks, dtype=jnp.int32) * block_rows
    return lax.map(jax.checkpoint(one_block), (grouped, offsets)).reshape(seq_len, H * HD)

def residual_block(inputs_seq, gain_attn, w_query, w_key, w_value, w_out, gain_moe, w_router, w_gate, w_up, w_down, routes_seq):
    seq_len = inputs_seq.shape[0]
    cosine, sine = rope_tables(seq_len, HD)
    normed_one = low(rms_scale(inputs_seq) * gain_attn)
    query_proj = low_back(matmul(normed_one, w_query))
    key_proj = low_back(matmul(normed_one, w_key))
    value_proj = low(low_back(matmul(normed_one, w_value)))
    query_rot = low(rotate(query_proj.reshape(seq_len, H, HD), cosine, sine))
    key_rot = low(rotate(key_proj.reshape(seq_len, KV, HD), cosine, sine))
    attn_out = low(low_back(attend(query_rot, key_rot, value_proj.reshape(seq_len, KV, HD))))
    hidden_mid = inputs_seq + low_back(matmul(attn_out, w_out))
    normed_two = low(rms_scale(hidden_mid) * gain_moe)
    logits = matmul(normed_two, w_router)
    gate_probs = jax.nn.softmax(jnp.take_along_axis(logits, routes_seq, axis=1), axis=-1)
    slot_index = slot_table(routes_seq)
    token_of = jnp.arange(seq_len * TOP, dtype=jnp.int32) // TOP
    dispatched = jnp.zeros((E * CAP, D), jnp.float32).at[slot_index].set(normed_two[token_of])
    groups = E // 8

    def expert_group(group_item):
        rows_in, gate_blk, up_blk, down_blk = group_item
        gate_h = low_back(jnp.einsum('ecd,efd->ecf', rows_in, gate_blk, precision=highest))
        up_h = low_back(jnp.einsum('ecd,efd->ecf', rows_in, up_blk, precision=highest))
        hidden_h = low(jax.nn.silu(gate_h) * up_h)
        return low_back(jnp.einsum('ecf,efd->ecd', hidden_h, down_blk, precision=highest))
    expert_out = lax.map(jax.checkpoint(expert_group), (dispatched.reshape(groups, 8, CAP, D), w_gate.reshape(groups, 8, FF, D), w_up.reshape(groups, 8, FF, D), w_down.reshape(groups, 8, FF, D))).reshape(E * CAP, D)
    picked = expert_out[slot_index].reshape(seq_len, TOP, D)
    mixture = low_back(lax.optimization_barrier(jnp.sum(picked * gate_probs[:, :, None], axis=1)))
    return hidden_mid + mixture

def reference(inputs, gain_attn, w_query, w_key, w_value, w_out, gain_moe, w_router, w_gate, w_up, w_down, routes, cotangent):
    weights = tuple((wt.astype(jnp.float32) for wt in (gain_attn, w_query, w_key, w_value, w_out, gain_moe, w_router, w_gate, w_up, w_down)))
    inputs_all = inputs.astype(jnp.float32).reshape(N_DP, SEQ, D)
    cot_all = cotangent.astype(jnp.float32).reshape(N_DP, SEQ, D)
    routes_all = routes.reshape(N_DP, SEQ, TOP)

    def one_sequence(totals, seq_item):
        inputs_seq, cot_seq, routes_seq = seq_item
        result, pullback = jax.vjp(lambda first, *rest: residual_block(first, *rest, routes_seq), inputs_seq, *weights)
        grads = pullback(cot_seq)
        return (tuple((acc + new for acc, new in zip(totals, grads[1:]))), (result.astype(jnp.bfloat16), grads[0]))
    zero_grads = tuple((jnp.zeros_like(wt) for wt in weights))
    totals, (outputs, input_grad) = lax.scan(one_sequence, zero_grads, (inputs_all, cot_all, routes_all))
    return (outputs.reshape(TOKENS, D), input_grad.reshape(TOKENS, D), totals[0], totals[1], totals[2], totals[3], totals[4], totals[5], totals[6], totals[7], totals[8], totals[9])
```

```python
import functools

import jax
import jax.numpy as jnp
from jax import lax
from jax.experimental import pallas as pl
from jax.experimental.pallas import tpu as pltpu
from jax.sharding import PartitionSpec as P

D = 1536
HD = 64
E = 40
TOP = 8
GROUPS = 5
RINGED = 3
TILES = 4
HOPS = (
    (),
    ((0, 1),),
    ((0, 1), (1, 1)),
    ((0, 1), (1, 1), (2, 1)),
    ((0, 1), (1, 1), (2, 1)),
    ((1, 1), (2, 2)),
)
BLOCK = 256
RING = (0, 2, 4, 6, 7, 5, 3, 1)


epsilon = 1e-06
contract_last = (((1,), (1,)), ((), ()))
contract_first = (((0,), (0,)), ((), ()))


def rope_tables(seq_len, width):
    position = jnp.arange(seq_len).astype(jnp.float32)
    freq = 10000.0 ** (-jnp.arange(width // 2).astype(jnp.float32) * 2.0 / width)
    angle = position[:, None] * freq[None, :]
    return (jnp.cos(angle)[:, None, :], jnp.sin(angle)[:, None, :])


def rotate(values, cosine, sine):
    half = values.shape[-1] // 2
    first_half = values[..., :half]
    second_half = values[..., half:]
    return jnp.concatenate(
        [first_half * cosine - second_half * sine, second_half * cosine + first_half * sine],
        axis=-1,
    )


def unrotate(grads, cosine, sine):
    half = grads.shape[-1] // 2
    first_half = grads[..., :half]
    second_half = grads[..., half:]
    return jnp.concatenate(
        [first_half * cosine + second_half * sine, second_half * cosine - first_half * sine],
        axis=-1,
    )


def rms_factor(values):
    return lax.rsqrt(jnp.mean(values * values, axis=-1, keepdims=True) + epsilon)


def norm_backward(values, factor, gain_f, normed_grad):
    weighted = normed_grad * gain_f
    values_grad = factor * weighted - values * factor**3 * jnp.mean(
        values * weighted, axis=-1, keepdims=True
    )
    return (values_grad, jnp.sum(normed_grad * values * factor, axis=0))


def block_scores(query_blk, key_rot, offset):
    rows, keys = query_blk.shape[0], key_rot.shape[0]
    scores = jnp.einsum(
        "qcgd,kcd->cgqk", query_blk, key_rot, preferred_element_type=jnp.float32
    ) * HD ** (-0.5)
    causal = (offset + jnp.arange(rows, dtype=jnp.int32))[:, None] >= jnp.arange(
        keys, dtype=jnp.int32
    )[None, :]
    return jnp.where(causal, scores, -1e30)


def attention_forward(query_rot, key_rot, value_hd):
    seq_len, heads, width = query_rot.shape
    kv_heads = key_rot.shape[1]
    block_rows = min(BLOCK, seq_len)
    grouped = query_rot.reshape(seq_len, kv_heads, heads // kv_heads, width)
    outs, logs = [], []
    for start in range(0, seq_len, block_rows):
        stop = start + block_rows
        scores = block_scores(grouped[start:stop], key_rot[:stop], start)
        highest_score = jnp.max(scores, axis=-1, keepdims=True)
        expo = jnp.exp(scores - highest_score)
        total = jnp.sum(expo, axis=-1, keepdims=True)
        prob_low = (expo / total).astype(jnp.bfloat16)
        attn_blk = jnp.einsum(
            "cgqk,kcd->qcgd", prob_low, value_hd[:stop], preferred_element_type=jnp.float32
        )
        outs.append(attn_blk.astype(jnp.bfloat16).reshape(block_rows, heads * width))
        logs.append((highest_score + jnp.log(total))[..., 0])
    return jnp.concatenate(outs, axis=0), logs


def attention_backward(query_rot, key_rot, value_hd, logs, out_grad_all):
    seq_len, heads, width = query_rot.shape
    kv_heads = key_rot.shape[1]
    block_rows = min(BLOCK, seq_len)
    grouped = query_rot.reshape(seq_len, kv_heads, heads // kv_heads, width)
    grad_groups = out_grad_all.reshape(grouped.shape)
    query_grads = []
    key_acc = jnp.zeros((seq_len, kv_heads, width), jnp.float32)
    value_acc = key_acc
    for number, start in enumerate(range(0, seq_len, block_rows)):
        stop = start + block_rows
        query_blk, grad_blk = grouped[start:stop], grad_groups[start:stop]
        keys, values = key_rot[:stop], value_hd[:stop]
        scores = block_scores(query_blk, keys, start)
        attn_prob = jnp.exp(scores - logs[number][..., None])
        prob_low = attn_prob.astype(jnp.bfloat16)
        prob_grad = jnp.einsum(
            "qcgd,kcd->cgqk", grad_blk, values, preferred_element_type=jnp.float32
        )
        score_grad = (
            attn_prob * (prob_grad - jnp.sum(attn_prob * prob_grad, axis=-1, keepdims=True))
        ).astype(jnp.bfloat16)
        query_grad = jnp.einsum(
            "cgqk,kcd->qcgd", score_grad, keys, preferred_element_type=jnp.float32
        ) * HD ** (-0.5)
        key_part = jnp.einsum(
            "cgqk,qcgd->kcd", score_grad, query_blk, preferred_element_type=jnp.float32
        ) * HD ** (-0.5)
        value_part = jnp.einsum(
            "cgqk,qcgd->kcd", prob_low, grad_blk, preferred_element_type=jnp.float32
        )
        rest = ((0, seq_len - stop), (0, 0), (0, 0))
        key_acc = key_acc + jnp.pad(key_part, rest)
        value_acc = value_acc + jnp.pad(value_part, rest)
        query_grads.append(query_grad.reshape(block_rows, heads, width))
    return jnp.concatenate(query_grads, axis=0), key_acc, value_acc


def swap(values, axis):
    return lax.ppermute(values, axis, [(0, 1), (1, 0)])


def gather_ordered(values):
    if lax.axis_size("tensor") != 2:
        return lax.all_gather(values, "tensor", axis=0, tiled=True)
    other = swap(values, "tensor")
    first = lax.axis_index("tensor") == 0
    return jnp.concatenate(
        [jnp.where(first, values, other), jnp.where(first, other, values)], axis=0
    )


def gather_rows(values):
    if lax.axis_size("tensor") == 2:
        sequence = jnp.concatenate([values, swap(values, "tensor")], axis=0)
    else:
        sequence = lax.all_gather(values, "tensor", axis=0, tiled=True)
    return jnp.concatenate([sequence, swap(sequence, "core")], axis=0)


def scatter_tensor(values, ordered):
    if lax.axis_size("tensor") != 2:
        return lax.psum_scatter(values, "tensor", scatter_dimension=0, tiled=True).astype(
            jnp.float32
        )
    half = values.shape[0] // 2
    if ordered:
        first = lax.axis_index("tensor") == 0
        low, high = values[:half], values[half:]
        kept, given = jnp.where(first, low, high), jnp.where(first, high, low)
    else:
        kept, given = values[:half], values[half:]
    return kept.astype(jnp.float32) + swap(given, "tensor").astype(jnp.float32)


def scatter_rows(values):
    half = values.shape[0] // 2
    mine = values[:half].astype(jnp.float32) + swap(
        values[half:].astype(jnp.bfloat16), "core"
    ).astype(jnp.float32)
    return scatter_tensor(mine.astype(jnp.bfloat16), False)


def sequence_routes(routes, own_rows):
    if lax.axis_size("tensor") == 2:
        second = lax.axis_index("tensor") == 1
        low, high = routes[:own_rows], routes[own_rows:]
        routes = jnp.concatenate(
            [jnp.where(second, high, low), jnp.where(second, low, high)], axis=0
        )
    return jnp.concatenate([routes, swap(routes, "core")], axis=0)


def dense_gates(logits, routes):
    experts = jnp.arange(E, dtype=jnp.int32)
    used = jnp.any(routes[:, :, None] == experts[None, None, :], axis=1)
    top = jnp.max(jnp.where(used, logits, -jnp.inf), axis=-1, keepdims=True)
    expo = jnp.where(used, jnp.exp(jnp.minimum(logits - top, 0.0)), 0.0)
    return expo / jnp.sum(expo, axis=-1, keepdims=True)


class Ring:
    def __init__(self, grads, flip):
        self.grads, self.step, self.hop_number = grads, -1 if flip else 1, 0
        self.count = len(RING)
        self.rows = grads.shape[2] // self.count
        self.place = jnp.asarray([RING.index(chip) for chip in range(self.count)], jnp.int32)[
            lax.axis_index("chip")
        ]
        self.chips = jnp.asarray(RING, jnp.int32)
        far = self.count // 2
        self.state = (self.own(self.step * far), self.own(-self.step * (far - 1)))

    def own(self, ahead):
        at = (self.place + ahead + self.count) % self.count
        start = self.chips[at] * self.rows
        return lax.dynamic_slice_in_dim(self.grads, start, self.rows, 2)

    def send(self, block, way):
        pairs = [(RING[i], RING[(i + way) % self.count]) for i in range(self.count)]
        return lax.ppermute(block, "chip", pairs)

    def hop(self):
        self.hop_number += 1
        hop, far = self.hop_number, self.count // 2
        ahead, behind = self.state
        ahead = self.send(ahead, self.step)
        if hop < far:
            ahead = self.add(ahead, self.own(self.step * (far - hop)))
        if hop < far - 1:
            behind = self.add(
                self.send(behind, -self.step), self.own(-self.step * (far - 1 - hop))
            )
        elif hop == far - 1:
            behind = self.send(behind, -self.step)
        self.state = (ahead, behind)

    def add(self, block, own):
        return (block.astype(jnp.float32) + own.astype(jnp.float32)).astype(jnp.bfloat16)

    def result(self):
        ahead, behind = self.state
        return (
            self.own(0).astype(jnp.float32)
            + ahead.astype(jnp.float32)
            + behind.astype(jnp.float32)
        )


class Whole:
    def __init__(self, grads):
        self.state = lax.psum_scatter(
            grads, "chip", scatter_dimension=2, tiled=True
        )

    def hop(self):
        pass

    def result(self):
        return self.state.astype(jnp.float32)


def scatter_experts(grads, number):
    if number < RINGED and lax.axis_size("chip") == len(RING):
        return Ring(grads, number % 2 == 1)
    return Whole(grads)


def tie(values, sums):
    values, states = lax.optimization_barrier((values, [each.state for each in sums]))
    for each, state in zip(sums, states):
        each.state = state
    return values


def expert_kernel(first, core_ref, tokens_ref, cot_ref, gates_ref, weights_ref, *refs):
    if not first:
        mix_in, rows_in, *refs = refs
    mix_out, rows_out, gate_grad_ref, grads_ref, mix, rows, sums, in_sem, out_sem = refs
    step, steps = pl.program_id(0), pl.num_programs(0)
    size = tokens_ref.shape[0] // TILES
    width = tokens_ref.shape[1]
    gate_w, up_w, down_w = (weights_ref[k].reshape(-1, width) for k in range(3))
    pair = gate_w.shape[0]

    def arriving(tile, which):
        part = pl.ds(tile * size, size)
        source, target = ((mix_in, mix), (rows_in, rows))[which]
        return pltpu.make_async_copy(source.at[part], target.at[part], in_sem.at[which, tile])

    def leaving(tile, which):
        part = pl.ds(tile * size, size)
        source, target = ((mix, mix_out), (rows, rows_out))[which]
        return pltpu.make_async_copy(source.at[part], target.at[part], out_sem.at[which, tile])

    def dot(left, right, contract):
        return lax.dot_general(
            left, right, (contract, ((), ())), preferred_element_type=jnp.float32
        )

    if not first:

        @pl.when(step == 0)
        def _():
            for tile in range(TILES):
                arriving(tile, 0).start()
                arriving(tile, 1).start()

    sums[...] = jnp.zeros_like(sums)

    def one_tile(tile, carry):
        part = pl.ds(pl.multiple_of(tile * size, size), size)
        tokens, cot = tokens_ref[part, :], cot_ref[part, :]
        gate_h = dot(gate_w, tokens, ((1,), (1,)))
        up_h = dot(up_w, tokens, ((1,), (1,)))
        cot_h = dot(down_w, cot, ((1,), (1,)))
        gates = jnp.broadcast_to(
            gates_ref[0, :, part][:, None, :], (2, pair // 2, size)
        ).reshape(pair, size)
        sigma = jax.nn.sigmoid(gate_h)
        silu = gate_h * sigma
        hidden_h = silu * up_h
        gate_grad_ref[0, :, part] = jnp.sum((hidden_h * cot_h).reshape(2, pair // 2, size), axis=1)
        weighted = (gates * hidden_h).astype(jnp.bfloat16)
        hidden_grad = gates * cot_h
        gate_hg = (hidden_grad * up_h * (sigma + silu * (1.0 - sigma))).astype(jnp.bfloat16)
        up_hg = (hidden_grad * silu).astype(jnp.bfloat16)

        @pl.when(step == 0)
        def _():
            if first:
                mix[part, :] = jnp.zeros((size, width), jnp.float32)
                rows[part, :] = jnp.zeros((size, width), jnp.float32)
            else:
                arriving(tile, 0).wait()
                arriving(tile, 1).wait()

        mix[part, :] += dot(weighted, down_w, ((0,), (0,)))
        rows[part, :] += dot(gate_hg, gate_w, ((0,), (0,))) + dot(up_hg, up_w, ((0,), (0,)))
        sums[0] += dot(gate_hg, tokens, ((1,), (0,)))
        sums[1] += dot(up_hg, tokens, ((1,), (0,)))
        sums[2] += dot(weighted, cot, ((1,), (0,)))

        @pl.when(step == steps - 1)
        def _():
            leaving(tile, 0).start()
            leaving(tile, 1).start()

        return carry

    lax.fori_loop(0, TILES, one_tile, 0)
    grads_ref[...] = sums[...].astype(jnp.bfloat16).reshape(grads_ref.shape)

    @pl.when(step == steps - 1)
    def _():
        for tile in range(TILES):
            leaving(tile, 0).wait()
            leaving(tile, 1).wait()


def expert_call(tokens, cot, gates, gathered, totals):
    first = totals is None
    count, width = tokens.shape
    _, each, chips, cores, shard, _ = gathered.shape
    pair = 2 * chips * shard
    core = lax.axis_index("core").astype(jnp.int32)[None]
    gates = gates.T.reshape(each // 2, 2, count)
    whole = pl.BlockSpec((count, width), lambda i, core: (0, 0), pipeline_mode=pl.Buffered(1))
    by_pair = pl.BlockSpec((1, 2, count), lambda i, core: (i, 0, 0))
    anywhere = pl.BlockSpec(memory_space=pl.ANY)
    total = jax.ShapeDtypeStruct((count, width), jnp.float32)
    mix, rows, gate_grad, grads = pl.pallas_call(
        functools.partial(expert_kernel, first),
        grid_spec=pltpu.PrefetchScalarGridSpec(
            num_scalar_prefetch=1,
            grid=(each // 2,),
            in_specs=[
                whole,
                whole,
                by_pair,
                pl.BlockSpec(
                    (3, 2, chips, None, shard, width), lambda i, core: (0, i, 0, core[0], 0, 0)
                ),
            ]
            + ([] if first else [anywhere, anywhere]),
            out_specs=[
                anywhere,
                anywhere,
                by_pair,
                pl.BlockSpec((3, 2, chips * shard, width), lambda i, core: (0, i, 0, 0)),
            ],
            scratch_shapes=[
                pltpu.VMEM((count, width), jnp.float32),
                pltpu.VMEM((count, width), jnp.float32),
                pltpu.VMEM((3, pair, width), jnp.float32),
                pltpu.SemaphoreType.DMA((2, TILES)),
                pltpu.SemaphoreType.DMA((2, TILES)),
            ],
        ),
        out_shape=[
            total,
            total,
            jax.ShapeDtypeStruct(gates.shape, jnp.float32),
            jax.ShapeDtypeStruct((3, each, chips * shard, width), jnp.bfloat16),
        ],
        input_output_aliases={} if first else {5: 0, 6: 1},
        compiler_params=pltpu.CompilerParams(vmem_limit_bytes=67043328),
        cost_estimate=pl.CostEstimate(
            flops=9 * count * width * pair * each,
            bytes_accessed=4 * 4 * count * width + 12 * each * chips * shard * width,
            transcendentals=count * pair * each // 2,
        ),
        name="experts",
    )(core, tokens, cot, gates, gathered, *(() if first else totals))
    return mix, rows, gate_grad.reshape(each, count).T, grads


def expert_group(tokens, cot, gates, gate_w, up_w, down_w):
    rows = tokens.shape[0]
    count, hidden = gate_w.shape[:2]
    flat = (count * hidden, D)
    gate_w, up_w, down_w = gate_w.reshape(flat), up_w.reshape(flat), down_w.reshape(flat)
    wide = jnp.broadcast_to(gates[:, :, None], (rows, count, hidden)).reshape(rows, -1)
    gate_h = lax.dot_general(tokens, gate_w, contract_last, preferred_element_type=jnp.float32)
    up_h = lax.dot_general(tokens, up_w, contract_last, preferred_element_type=jnp.float32)
    cot_h = lax.dot_general(cot, down_w, contract_last, preferred_element_type=jnp.float32)
    sigma = jax.nn.sigmoid(gate_h)
    silu = gate_h * sigma
    hidden_h = silu * up_h
    gate_grad = jnp.sum((hidden_h * cot_h).reshape(rows, count, hidden), axis=-1)
    hidden_grad = wide * cot_h
    weighted = (wide * hidden_h).astype(jnp.bfloat16)
    gate_hg = (hidden_grad * up_h * sigma * (1.0 + gate_h * (1.0 - sigma))).astype(jnp.bfloat16)
    up_hg = (hidden_grad * silu).astype(jnp.bfloat16)
    mixture = jnp.dot(weighted, down_w, preferred_element_type=jnp.float32)
    rows_grad = jnp.dot(gate_hg, gate_w, preferred_element_type=jnp.float32) + jnp.dot(
        up_hg, up_w, preferred_element_type=jnp.float32
    )
    grads = jnp.stack([
        lax.dot_general(left, right, contract_first, preferred_element_type=jnp.float32)
        .astype(jnp.bfloat16)
        .reshape(count, hidden, D)
        for left, right in ((gate_hg, tokens), (up_hg, tokens), (weighted, cot))
    ])
    return mixture, rows_grad, gate_grad, grads


def body(
    inputs,
    gain_attn,
    w_query,
    w_key,
    w_value,
    w_out,
    gain_moe,
    w_router,
    w_gate,
    w_up,
    w_down,
    routes,
    cotangent,
):
    parts = lax.axis_size("tensor")
    own_rows = inputs.shape[0]
    seq_len = own_rows * parts
    cosine, sine = rope_tables(seq_len, HD)
    inputs_f = inputs.astype(jnp.float32)
    q_cols, k_cols = w_query.shape[1], w_key.shape[1]
    proj_cols = q_cols + 2 * k_cols
    filler = jnp.zeros((w_query.shape[0], 127), jnp.bfloat16)
    packed = jnp.concatenate([w_query, w_key, w_value, gain_attn[:, None], filler], axis=1)
    packed = lax.all_gather(packed, ("chip", "core"), axis=0, tiled=True)
    proj_w, gain_one_f = packed[:, :proj_cols], packed[:, proj_cols].astype(jnp.float32)
    query_w, key_w, value_w = jnp.split(proj_w, [q_cols, q_cols + k_cols], axis=1)
    packed = jnp.concatenate(
        [w_out.T, w_router, gain_moe[:, None], filler[:, : 127 - E]], axis=1
    )
    packed, _ = lax.optimization_barrier((packed, proj_w))
    packed = lax.all_gather(packed, ("chip", "core"), axis=0, tiled=True)
    out_wt, router_w = packed[:, :q_cols], packed[:, q_cols : q_cols + E]
    gain_two_f = packed[:, q_cols + E].astype(jnp.float32)

    shard = w_gate.shape[1] // D
    groups = GROUPS
    each = E // groups
    stacked = [w.reshape(E, shard, D) for w in (w_gate, w_up, w_down)]
    gathered = []
    for g in range(groups):
        part = jnp.stack([w[g * each : (g + 1) * each] for w in stacked])
        gathered.append(lax.all_gather(part, ("chip", "core"), axis=2, tiled=True))

    cot_rows = gather_rows(cotangent)
    routes_rows = sequence_routes(routes, own_rows)

    scale_one = rms_factor(inputs_f)
    normed_one = (inputs_f * scale_one * gain_one_f).astype(jnp.bfloat16)
    normed_all = gather_ordered(normed_one)
    query_proj = jnp.dot(normed_all, query_w, preferred_element_type=jnp.float32)
    key_proj = jnp.dot(normed_all, key_w, preferred_element_type=jnp.float32)
    value_proj = jnp.dot(normed_all, value_w, preferred_element_type=jnp.float32)
    query_rot = rotate(query_proj.reshape(seq_len, -1, HD), cosine, sine).astype(jnp.bfloat16)
    key_rot = rotate(key_proj.reshape(seq_len, -1, HD), cosine, sine).astype(jnp.bfloat16)
    value_hd = value_proj.reshape(seq_len, -1, HD).astype(jnp.bfloat16)
    attn_out, log_total = attention_forward(query_rot, key_rot, value_hd)
    hidden_mid = inputs_f + scatter_tensor(
        lax.dot_general(
            attn_out, out_wt, contract_last, preferred_element_type=jnp.float32
        ).astype(jnp.bfloat16),
        True,
    )
    scale_two = rms_factor(hidden_mid)
    normed_two = (hidden_mid * scale_two * gain_two_f).astype(jnp.bfloat16)
    token_rows = gather_rows(normed_two)
    logits = jnp.dot(token_rows, router_w, preferred_element_type=jnp.float32)
    gates = dense_gates(logits, routes_rows)

    mixture, rows_grad, gate_grads, expert_sums = 0.0, 0.0, [], []
    for g in range(groups):
        token_rows_g, cot_rows_g = token_rows, cot_rows
        if g > 0:
            for done, hops in HOPS[g - 1]:
                for _ in range(hops):
                    expert_sums[done].hop()
            token_rows_g, cot_rows_g, mixture, rows_grad, grads, gathered[g] = tie(
                (token_rows, cot_rows, mixture, rows_grad, grads, gathered[g]),
                [expert_sums[done] for done, _ in HOPS[g - 1]],
            )
            expert_sums.append(scatter_experts(grads, g - 1))
        by_core = gathered[g].reshape(3, each, -1, 2, shard, D)
        group_gates = gates[:, g * each : (g + 1) * each]
        if shard == 16 and by_core.shape[2] == 8:
            mixture, rows_grad, gate_grad, grads = expert_call(
                token_rows_g,
                cot_rows_g,
                group_gates,
                by_core,
                (mixture, rows_grad) if g > 0 else None,
            )
        else:
            by_core = lax.dynamic_index_in_dim(by_core, lax.axis_index("core"), 3, keepdims=False)
            gate_w, up_w, down_w = by_core.reshape(3, each, -1, D)
            mix, rows, gate_grad, grads = expert_group(
                token_rows_g, cot_rows_g, group_gates, gate_w, up_w, down_w
            )
            mixture, rows_grad = mixture + mix, rows_grad + rows
        gate_grads.append(gate_grad)
    for done, hops in HOPS[groups - 1]:
        for _ in range(hops):
            expert_sums[done].hop()
    mixture, rows_grad, grads = tie(
        (mixture, rows_grad, grads), [expert_sums[done] for done, _ in HOPS[groups - 1]]
    )
    expert_sums.append(scatter_experts(grads, groups - 1))
    outputs = (hidden_mid + scatter_rows(mixture)).astype(jnp.bfloat16)
    normed_grad = scatter_rows(rows_grad)
    gate_grad_own = scatter_rows(jnp.concatenate(gate_grads, axis=1))
    if parts == 2:
        probs_own = gates[:own_rows]
    else:
        probs_own = lax.dynamic_slice_in_dim(
            gates, lax.axis_index("tensor") * own_rows, own_rows, 0
        )
    logit_grad = (
        probs_own * (gate_grad_own - jnp.sum(probs_own * gate_grad_own, axis=-1, keepdims=True))
    ).astype(jnp.bfloat16)
    normed_grad = normed_grad + lax.dot_general(
        logit_grad, router_w, contract_last, preferred_element_type=jnp.float32
    )
    router_grad = lax.dot_general(
        normed_two,
        jnp.pad(logit_grad, ((0, 0), (0, 128 - E))),
        contract_first,
        preferred_element_type=jnp.float32,
    )
    mid_part, gain_two_grad = norm_backward(hidden_mid, scale_two, gain_two_f, normed_grad)
    mid_grad = cotangent.astype(jnp.float32) + mid_part
    mid_all = gather_ordered(mid_grad.astype(jnp.bfloat16))
    for done, hops in HOPS[groups]:
        for _ in range(hops):
            expert_sums[done].hop()
    out_wt_grad = lax.dot_general(
        mid_all, attn_out, contract_first, preferred_element_type=jnp.float32
    )
    attn_out_grad = jnp.dot(mid_all, out_wt, preferred_element_type=jnp.float32).astype(
        jnp.bfloat16
    )
    query_grad, key_grad, value_grad = attention_backward(
        query_rot, key_rot, value_hd, log_total, attn_out_grad
    )
    query_pg = unrotate(query_grad, cosine, sine).reshape(seq_len, -1).astype(jnp.bfloat16)
    key_pg = unrotate(key_grad, cosine, sine).reshape(seq_len, -1).astype(jnp.bfloat16)
    value_pg = value_grad.reshape(seq_len, -1).astype(jnp.bfloat16)
    proj_pg = jnp.concatenate([query_pg, key_pg, value_pg], axis=1)
    proj_w_grad = lax.dot_general(
        normed_all, proj_pg, contract_first, preferred_element_type=jnp.float32
    )
    normed_one_grad = scatter_tensor(
        lax.dot_general(
            proj_pg, proj_w, contract_last, preferred_element_type=jnp.float32
        ).astype(jnp.bfloat16),
        True,
    )
    input_part, gain_one_grad = norm_backward(inputs_f, scale_one, gain_one_f, normed_one_grad)
    input_grad = mid_grad + input_part
    column = jnp.arange(128, dtype=jnp.int32)[None, :]
    small_grad = jnp.where(
        column < E,
        router_grad,
        jnp.where(
            column == E,
            gain_one_grad[:, None],
            jnp.where(column == E + 1, gain_two_grad[:, None], 0.0),
        ),
    )
    sums = jnp.concatenate(
        [
            proj_w_grad.astype(jnp.bfloat16),
            out_wt_grad.astype(jnp.bfloat16),
            small_grad.astype(jnp.bfloat16),
        ],
        axis=1,
    )
    sums = tie(sums, expert_sums)
    sums = lax.psum_scatter(
        sums, ("chip", "core"), scatter_dimension=0, tiled=True
    ).astype(jnp.float32)
    shared = sums[:, proj_cols + q_cols :]
    if parts == 2:
        shared = shared + swap(shared, "tensor")
    else:
        shared = lax.psum(shared, "tensor")
    expert_grads = jnp.concatenate([each.result() for each in expert_sums], axis=1)
    expert_grads = expert_grads.reshape(3, E, shard * D)
    return (
        outputs,
        input_grad,
        shared[:, E],
        sums[:, :q_cols],
        sums[:, q_cols : q_cols + k_cols],
        sums[:, q_cols + k_cols : proj_cols],
        sums[:, proj_cols : proj_cols + q_cols].T,
        shared[:, E + 1],
        shared[:, :E],
        expert_grads[0],
        expert_grads[1],
        expert_grads[2],
    )


def solution(mesh):
    dp, parts = mesh.devices.shape
    cores = jax.sharding.Mesh(mesh.devices.reshape(dp // 2, 2, parts), ("chip", "core", "tensor"))
    dp = ("chip", "core")
    every = ("chip", "core", "tensor")
    in_specs = (
        P(every, None),
        P(dp),
        P(dp, "tensor"),
        P(dp, "tensor"),
        P(dp, "tensor"),
        P("tensor", dp),
        P(dp),
        P(dp, None),
        P(None, every),
        P(None, every),
        P(None, every),
        P(dp, None),
        P(every, None),
    )
    out_specs = (
        P(every, None),
        P(every, None),
        P(dp),
        P(dp, "tensor"),
        P(dp, "tensor"),
        P(dp, "tensor"),
        P("tensor", dp),
        P(dp),
        P(dp, None),
        P(None, every),
        P(None, every),
        P(None, every),
    )
    return jax.shard_map(body, mesh=cores, in_specs=in_specs, out_specs=out_specs, check_vma=False)
```

```python
import functools

import jax
import jax.numpy as jnp
from jax import lax
from jax.experimental import pallas as pl
from jax.experimental.pallas import tpu as pltpu
from jax.sharding import PartitionSpec as P


D = 1536
HD = 64
E = 40
GROUPS = 5
RINGED = 5
TILES = 4
HOPS = (
    (),
    (),
    (),
    (),
    ((0, 1), (1, 1), (2, 1)),
    ((0, 1), (1, 1), (2, 1), (3, 1)),
    ((0, 1), (1, 1), (2, 1), (3, 1), (4, 1)),
    ((0, 1), (1, 1)),
    ((2, 1), (3, 2), (4, 3)),
)
BLOCK = 256
RING = (0, 2, 4, 6, 7, 5, 3, 1)


epsilon = 1e-06
contract_last = (((1,), (1,)), ((), ()))
contract_first = (((0,), (0,)), ((), ()))


def rope_tables(seq_len, width):
    position = jnp.arange(seq_len).astype(jnp.float32)
    freq = 10000.0 ** (-jnp.arange(width // 2).astype(jnp.float32) * 2.0 / width)
    angle = position[:, None] * freq[None, :]
    return (jnp.cos(angle)[:, None, :], jnp.sin(angle)[:, None, :])


def rotate(values, cosine, sine):
    half = values.shape[-1] // 2
    first_half = values[..., :half]
    second_half = values[..., half:]
    return jnp.concatenate(
        [first_half * cosine - second_half * sine, second_half * cosine + first_half * sine],
        axis=-1,
    )


def unrotate(grads, cosine, sine):
    half = grads.shape[-1] // 2
    first_half = grads[..., :half]
    second_half = grads[..., half:]
    return jnp.concatenate(
        [first_half * cosine + second_half * sine, second_half * cosine - first_half * sine],
        axis=-1,
    )


def rms_factor(values):
    return lax.rsqrt(jnp.mean(values * values, axis=-1, keepdims=True) + epsilon)


def norm_backward(values, factor, gain_f, normed_grad):
    weighted = normed_grad * gain_f
    values_grad = factor * weighted - values * factor**3 * jnp.mean(
        values * weighted, axis=-1, keepdims=True
    )
    return (values_grad, jnp.sum(normed_grad * values * factor, axis=0))


def block_scores(query_blk, key_rot, offset):
    rows, keys = query_blk.shape[0], key_rot.shape[0]
    scores = jnp.einsum(
        "qcgd,kcd->cgqk", query_blk, key_rot, preferred_element_type=jnp.float32
    ) * HD ** (-0.5)
    causal = (offset + jnp.arange(rows, dtype=jnp.int32))[:, None] >= jnp.arange(
        keys, dtype=jnp.int32
    )[None, :]
    return jnp.where(causal, scores, -1e30)


def attention_forward(query_rot, key_rot, value_hd):
    seq_len, heads, width = query_rot.shape
    kv_heads = key_rot.shape[1]
    block_rows = min(BLOCK, seq_len)
    grouped = query_rot.reshape(seq_len, kv_heads, heads // kv_heads, width)
    blocks = seq_len // block_rows
    half = max(1, blocks // 2)
    outs, logs = [None] * blocks, [None] * blocks
    for number in [block for first in range(half) for block in range(first, blocks, half)]:
        start, stop = number * block_rows, (number + 1) * block_rows
        scores = block_scores(grouped[start:stop], key_rot[:stop], start)
        highest_score = jnp.max(scores, axis=-1, keepdims=True)
        expo = jnp.exp(scores - highest_score)
        total = jnp.sum(expo, axis=-1, keepdims=True)
        prob_low = (expo / total).astype(jnp.bfloat16)
        attn_blk = jnp.einsum(
            "cgqk,kcd->qcgd", prob_low, value_hd[:stop], preferred_element_type=jnp.float32
        )
        outs[number] = attn_blk.astype(jnp.bfloat16).reshape(block_rows, heads * width)
        logs[number] = (highest_score + jnp.log(total))[..., 0]
        if number == blocks - half and half > 1:
            key_rot, value_hd, outs[0], outs[number] = lax.optimization_barrier(
                (key_rot, value_hd, outs[0], outs[number])
            )
    return outs, logs


def attention_backward(query_rot, key_rot, value_hd, logs, out_grad_all):
    seq_len, heads, width = query_rot.shape
    kv_heads = key_rot.shape[1]
    block_rows = min(BLOCK, seq_len)
    grouped = query_rot.reshape(seq_len, kv_heads, heads // kv_heads, width)
    grad_groups = out_grad_all.reshape(grouped.shape)
    query_grads = []
    key_acc = jnp.zeros((seq_len, kv_heads, width), jnp.float32)
    value_acc = key_acc
    for number, start in enumerate(range(0, seq_len, block_rows)):
        stop = start + block_rows
        query_blk, grad_blk = grouped[start:stop], grad_groups[start:stop]
        keys, values = key_rot[:stop], value_hd[:stop]
        scores = block_scores(query_blk, keys, start)
        attn_prob = jnp.exp(scores - logs[number][..., None])
        prob_low = attn_prob.astype(jnp.bfloat16)
        prob_grad = jnp.einsum(
            "qcgd,kcd->cgqk", grad_blk, values, preferred_element_type=jnp.float32
        )
        score_grad = (
            attn_prob * (prob_grad - jnp.sum(attn_prob * prob_grad, axis=-1, keepdims=True))
        ).astype(jnp.bfloat16)
        query_grad = jnp.einsum(
            "cgqk,kcd->qcgd", score_grad, keys, preferred_element_type=jnp.float32
        ) * HD ** (-0.5)
        key_part = jnp.einsum(
            "cgqk,qcgd->kcd", score_grad, query_blk, preferred_element_type=jnp.float32
        ) * HD ** (-0.5)
        value_part = jnp.einsum(
            "cgqk,qcgd->kcd", prob_low, grad_blk, preferred_element_type=jnp.float32
        )
        rest = ((0, seq_len - stop), (0, 0), (0, 0))
        key_acc = key_acc + jnp.pad(key_part, rest)
        value_acc = value_acc + jnp.pad(value_part, rest)
        query_grads.append(query_grad.reshape(block_rows, heads, width))
    return jnp.concatenate(query_grads, axis=0), key_acc, value_acc


def swap(values, axis):
    return lax.ppermute(values, axis, [(0, 1), (1, 0)])


def gather_ordered(values):
    if lax.axis_size("tensor") != 2:
        return lax.all_gather(values, "tensor", axis=0, tiled=True)
    other = swap(values, "tensor")
    first = lax.axis_index("tensor") == 0
    return jnp.concatenate(
        [jnp.where(first, values, other), jnp.where(first, other, values)], axis=0
    )


def gather_rows(values):
    if lax.axis_size("tensor") == 2:
        sequence = jnp.concatenate([values, swap(values, "tensor")], axis=0)
    else:
        sequence = lax.all_gather(values, "tensor", axis=0, tiled=True)
    return jnp.concatenate([sequence, swap(sequence, "core")], axis=0)


def scatter_tensor(values, ordered):
    if lax.axis_size("tensor") != 2:
        return lax.psum_scatter(values, "tensor", scatter_dimension=0, tiled=True).astype(
            jnp.float32
        )
    half = values.shape[0] // 2
    if ordered:
        first = lax.axis_index("tensor") == 0
        low, high = values[:half], values[half:]
        kept, given = jnp.where(first, low, high), jnp.where(first, high, low)
    else:
        kept, given = values[:half], values[half:]
    return kept.astype(jnp.float32) + swap(given, "tensor").astype(jnp.float32)


def scatter_rows(values):
    half = values.shape[0] // 2
    mine = values[:half].astype(jnp.float32) + swap(
        values[half:].astype(jnp.bfloat16), "core"
    ).astype(jnp.float32)
    return scatter_tensor(mine.astype(jnp.bfloat16), False)


def sequence_routes(routes, own_rows):
    if lax.axis_size("tensor") == 2:
        second = lax.axis_index("tensor") == 1
        low, high = routes[:own_rows], routes[own_rows:]
        routes = jnp.concatenate(
            [jnp.where(second, high, low), jnp.where(second, low, high)], axis=0
        )
    return jnp.concatenate([routes, swap(routes, "core")], axis=0)


def dense_gates(logits, routes):
    experts = jnp.arange(E, dtype=jnp.int32)
    used = jnp.any(routes[:, :, None] == experts[None, None, :], axis=1)
    top = jnp.max(jnp.where(used, logits, -jnp.inf), axis=-1, keepdims=True)
    expo = jnp.where(used, jnp.exp(jnp.minimum(logits - top, 0.0)), 0.0)
    return expo / jnp.sum(expo, axis=-1, keepdims=True)


class Ring:
    def __init__(self, grads, flip, starts):
        self.grads, self.step, self.hop_number = grads, -1 if flip else 1, 0
        self.count = len(RING)
        self.rows = grads.shape[2] // self.count
        self.starts = starts
        far = self.count // 2
        self.state = (self.own(self.step * far), self.own(-self.step * (far - 1)))

    def own(self, ahead):
        start = self.starts[ahead % self.count]
        return lax.dynamic_slice_in_dim(self.grads, start, self.rows, 2)

    def send(self, block, way):
        pairs = [(RING[i], RING[(i + way) % self.count]) for i in range(self.count)]
        return lax.ppermute(block, "chip", pairs)

    def hop(self):
        self.hop_number += 1
        hop, far = self.hop_number, self.count // 2
        ahead, behind = self.state
        ahead = self.send(ahead, self.step)
        if hop < far:
            ahead = self.add(ahead, self.own(self.step * (far - hop)))
        if hop < far - 1:
            behind = self.add(
                self.send(behind, -self.step), self.own(-self.step * (far - 1 - hop))
            )
        elif hop == far - 1:
            behind = self.send(behind, -self.step)
        self.state = (ahead, behind)

    def add(self, block, own):
        return (block.astype(jnp.float32) + own.astype(jnp.float32)).astype(jnp.bfloat16)

    def result(self):
        ahead, behind = self.state
        return (
            self.own(0).astype(jnp.float32)
            + ahead.astype(jnp.float32)
            + behind.astype(jnp.float32)
        )


class Whole:
    def __init__(self, grads):
        self.state = lax.psum_scatter(
            grads, "chip", scatter_dimension=2, tiled=True
        )

    def hop(self):
        pass

    def result(self):
        return self.state.astype(jnp.float32)


def ring_starts(rows):
    count = len(RING)
    if lax.axis_size("chip") != count:
        return None
    table = [[RING[(RING.index(c) + a) % count] * rows for a in range(count)] for c in range(count)]
    mine = jnp.asarray(table, jnp.int32)[lax.axis_index("chip")]
    return [mine[a] for a in range(count)]


def scatter_experts(grads, number, starts):
    if number < RINGED and starts is not None:
        return Ring(grads, number % 2 == 1, starts)
    return Whole(grads)


def run_hops(sums, stage):
    for which, count in HOPS[stage]:
        for _ in range(count):
            sums[which].hop()


def tie(values, sums):
    values, states = lax.optimization_barrier((values, [each.state for each in sums]))
    for each, state in zip(sums, states):
        each.state = state
    return values


def expert_kernel(first, core_ref, tokens_ref, cot_ref, gates_ref, weights_ref, *refs):
    if not first:
        mix_in, rows_in, *refs = refs
    mix_out, rows_out, gate_grad_ref, grads_ref, mix, rows, sums, in_sem, out_sem = refs
    step, steps = pl.program_id(0), pl.num_programs(0)
    size = tokens_ref.shape[0] // TILES
    width = tokens_ref.shape[1]
    gate_w, up_w, down_w = (weights_ref[k].reshape(-1, width) for k in range(3))
    pair = gate_w.shape[0]

    def arriving(tile, which):
        part = pl.ds(tile * size, size)
        source, target = ((mix_in, mix), (rows_in, rows))[which]
        return pltpu.make_async_copy(source.at[part], target.at[part], in_sem.at[which, tile])

    def leaving(tile, which):
        part = pl.ds(tile * size, size)
        source, target = ((mix, mix_out), (rows, rows_out))[which]
        return pltpu.make_async_copy(source.at[part], target.at[part], out_sem.at[which, tile])

    def dot(left, right, contract):
        return lax.dot_general(
            left, right, (contract, ((), ())), preferred_element_type=jnp.float32
        )

    if not first:

        @pl.when(step == 0)
        def _():
            for tile in range(TILES):
                arriving(tile, 0).start()
                arriving(tile, 1).start()

    sums[...] = jnp.zeros_like(sums)

    def one_tile(tile, carry):
        part = pl.ds(pl.multiple_of(tile * size, size), size)
        tokens, cot = tokens_ref[part, :], cot_ref[part, :]
        gate_h = dot(gate_w, tokens, ((1,), (1,)))
        up_h = dot(up_w, tokens, ((1,), (1,)))
        cot_h = dot(down_w, cot, ((1,), (1,)))
        gates = jnp.broadcast_to(
            gates_ref[0, :, part][:, None, :], (2, pair // 2, size)
        ).reshape(pair, size)
        sigma = jax.nn.sigmoid(gate_h)
        silu = gate_h * sigma
        hidden_h = silu * up_h
        gate_grad_ref[0, :, part] = jnp.sum((hidden_h * cot_h).reshape(2, pair // 2, size), axis=1)
        weighted = (gates * hidden_h).astype(jnp.bfloat16)
        hidden_grad = gates * cot_h
        gate_hg = (hidden_grad * up_h * (sigma + silu * (1.0 - sigma))).astype(jnp.bfloat16)
        up_hg = (hidden_grad * silu).astype(jnp.bfloat16)

        @pl.when(step == 0)
        def _():
            if first:
                mix[part, :] = jnp.zeros((size, width), jnp.float32)
                rows[part, :] = jnp.zeros((size, width), jnp.float32)
            else:
                arriving(tile, 0).wait()
                arriving(tile, 1).wait()

        mix[part, :] += dot(weighted, down_w, ((0,), (0,)))
        rows[part, :] += dot(gate_hg, gate_w, ((0,), (0,))) + dot(up_hg, up_w, ((0,), (0,)))
        sums[0] += dot(gate_hg, tokens, ((1,), (0,)))
        sums[1] += dot(up_hg, tokens, ((1,), (0,)))
        sums[2] += dot(weighted, cot, ((1,), (0,)))

        @pl.when(step == steps - 1)
        def _():
            leaving(tile, 0).start()
            leaving(tile, 1).start()

        return carry

    lax.fori_loop(0, TILES, one_tile, 0)
    grads_ref[...] = sums[...].astype(jnp.bfloat16).reshape(grads_ref.shape)

    @pl.when(step == steps - 1)
    def _():
        for tile in range(TILES):
            leaving(tile, 0).wait()
            leaving(tile, 1).wait()


def expert_call(tokens, cot, gates, gathered, totals):
    first = totals is None
    count, width = tokens.shape
    _, each, chips, _, shard, _ = gathered.shape
    pair = 2 * chips * shard
    core = lax.axis_index("core").astype(jnp.int32)[None]
    gates = gates.T.reshape(each // 2, 2, count)
    whole = pl.BlockSpec((count, width), lambda i, core: (0, 0), pipeline_mode=pl.Buffered(1))
    by_pair = pl.BlockSpec((1, 2, count), lambda i, core: (i, 0, 0))
    anywhere = pl.BlockSpec(memory_space=pl.ANY)
    total = jax.ShapeDtypeStruct((count, width), jnp.float32)
    mix, rows, gate_grad, grads = pl.pallas_call(
        functools.partial(expert_kernel, first),
        grid_spec=pltpu.PrefetchScalarGridSpec(
            num_scalar_prefetch=1,
            grid=(each // 2,),
            in_specs=[
                whole,
                whole,
                by_pair,
                pl.BlockSpec(
                    (3, 2, chips, None, shard, width), lambda i, core: (0, i, 0, core[0], 0, 0)
                ),
            ]
            + ([] if first else [anywhere, anywhere]),
            out_specs=[
                anywhere,
                anywhere,
                by_pair,
                pl.BlockSpec((3, 2, chips * shard, width), lambda i, core: (0, i, 0, 0)),
            ],
            scratch_shapes=[
                pltpu.VMEM((count, width), jnp.float32),
                pltpu.VMEM((count, width), jnp.float32),
                pltpu.VMEM((3, pair, width), jnp.float32),
                pltpu.SemaphoreType.DMA((2, TILES)),
                pltpu.SemaphoreType.DMA((2, TILES)),
            ],
        ),
        out_shape=[
            total,
            total,
            jax.ShapeDtypeStruct(gates.shape, jnp.float32),
            jax.ShapeDtypeStruct((3, each, chips * shard, width), jnp.bfloat16),
        ],
        input_output_aliases={} if first else {5: 0, 6: 1},
        compiler_params=pltpu.CompilerParams(vmem_limit_bytes=67043328),
        cost_estimate=pl.CostEstimate(
            flops=9 * count * width * pair * each,
            bytes_accessed=4 * 4 * count * width + 12 * each * chips * shard * width,
            transcendentals=count * pair * each // 2,
        ),
        name="experts",
    )(core, tokens, cot, gates, gathered, *(() if first else totals))
    return mix, rows, gate_grad.reshape(each, count).T, grads


def expert_group(tokens, cot, gates, gate_w, up_w, down_w):
    rows = tokens.shape[0]
    count, hidden = gate_w.shape[:2]
    flat = (count * hidden, D)
    gate_w, up_w, down_w = gate_w.reshape(flat), up_w.reshape(flat), down_w.reshape(flat)
    wide = jnp.broadcast_to(gates[:, :, None], (rows, count, hidden)).reshape(rows, -1)
    gate_h = lax.dot_general(tokens, gate_w, contract_last, preferred_element_type=jnp.float32)
    up_h = lax.dot_general(tokens, up_w, contract_last, preferred_element_type=jnp.float32)
    cot_h = lax.dot_general(cot, down_w, contract_last, preferred_element_type=jnp.float32)
    sigma = jax.nn.sigmoid(gate_h)
    silu = gate_h * sigma
    hidden_h = silu * up_h
    gate_grad = jnp.sum((hidden_h * cot_h).reshape(rows, count, hidden), axis=-1)
    hidden_grad = wide * cot_h
    weighted = (wide * hidden_h).astype(jnp.bfloat16)
    gate_hg = (hidden_grad * up_h * sigma * (1.0 + gate_h * (1.0 - sigma))).astype(jnp.bfloat16)
    up_hg = (hidden_grad * silu).astype(jnp.bfloat16)
    mixture = jnp.dot(weighted, down_w, preferred_element_type=jnp.float32)
    rows_grad = jnp.dot(gate_hg, gate_w, preferred_element_type=jnp.float32) + jnp.dot(
        up_hg, up_w, preferred_element_type=jnp.float32
    )
    grads = jnp.stack([
        lax.dot_general(left, right, contract_first, preferred_element_type=jnp.float32)
        .astype(jnp.bfloat16)
        .reshape(count, hidden, D)
        for left, right in ((gate_hg, tokens), (up_hg, tokens), (weighted, cot))
    ])
    return mixture, rows_grad, gate_grad, grads


def body(
    inputs,
    gain_attn,
    w_query,
    w_key,
    w_value,
    w_out,
    gain_moe,
    w_router,
    w_gate,
    w_up,
    w_down,
    routes,
    cotangent,
):
    parts = lax.axis_size("tensor")
    own_rows = inputs.shape[0]
    seq_len = own_rows * parts
    cosine, sine = rope_tables(seq_len, HD)
    inputs_f = inputs.astype(jnp.float32)
    q_cols, k_cols = w_query.shape[1], w_key.shape[1]
    proj_cols = q_cols + 2 * k_cols
    filler = jnp.zeros((w_query.shape[0], 127), jnp.bfloat16)
    packed = jnp.concatenate([w_query, w_key, w_value, gain_attn[:, None], filler], axis=1)
    packed = lax.all_gather(packed, ("chip", "core"), axis=0, tiled=True)
    proj_w, gain_one_f = packed[:, :proj_cols], packed[:, proj_cols].astype(jnp.float32)
    query_w, key_w, value_w = jnp.split(proj_w, [q_cols, q_cols + k_cols], axis=1)
    packed = jnp.concatenate(
        [w_out.T, w_router, gain_moe[:, None], filler[:, : 127 - E]], axis=1
    )
    packed, _ = lax.optimization_barrier((packed, proj_w))
    packed = lax.all_gather(packed, ("chip", "core"), axis=0, tiled=True)
    out_wt, router_w = packed[:, :q_cols], packed[:, q_cols : q_cols + E]
    gain_two_f = packed[:, q_cols + E].astype(jnp.float32)

    shard = w_gate.shape[1] // D
    starts = ring_starts(shard)
    groups = GROUPS
    each = E // groups
    stacked = [w.reshape(E, shard, D) for w in (w_gate, w_up, w_down)]
    gathered = []
    for g in range(groups):
        part = jnp.stack([w[g * each : (g + 1) * each] for w in stacked])
        gathered.append(lax.all_gather(part, ("chip", "core"), axis=2, tiled=True))

    inputs_all = gather_ordered(inputs)
    inputs_all, cot_later = lax.optimization_barrier((inputs_all, cotangent))
    cot_rows = gather_rows(cot_later)
    routes_rows = sequence_routes(routes, own_rows)

    scale_one = rms_factor(inputs_f)
    inputs_all = inputs_all.astype(jnp.float32)
    normed_all = (inputs_all * rms_factor(inputs_all) * gain_one_f).astype(jnp.bfloat16)
    query_proj = jnp.dot(normed_all, query_w, preferred_element_type=jnp.float32)
    key_proj = jnp.dot(normed_all, key_w, preferred_element_type=jnp.float32)
    value_proj = jnp.dot(normed_all, value_w, preferred_element_type=jnp.float32)
    query_rot = rotate(query_proj.reshape(seq_len, -1, HD), cosine, sine).astype(jnp.bfloat16)
    key_rot = rotate(key_proj.reshape(seq_len, -1, HD), cosine, sine).astype(jnp.bfloat16)
    value_hd = value_proj.reshape(seq_len, -1, HD).astype(jnp.bfloat16)
    attn_outs, log_total = attention_forward(query_rot, key_rot, value_hd)
    attn_out = jnp.concatenate(attn_outs, axis=0)
    chunks = len(attn_outs) // 2 if parts == 2 else 1
    piece = own_rows // chunks
    hidden_parts, scale_parts, normed_parts = [], [], []
    for c in range(chunks):
        both = jnp.concatenate([attn_outs[c], attn_outs[c + chunks]], axis=0) if parts == 2 else attn_out
        hidden_part = inputs_f[c * piece : (c + 1) * piece] + scatter_tensor(
            lax.dot_general(
                both, out_wt, contract_last, preferred_element_type=jnp.float32
            ).astype(jnp.bfloat16),
            True,
        )
        scale_part = rms_factor(hidden_part)
        hidden_parts.append(hidden_part)
        scale_parts.append(scale_part)
        normed_parts.append((hidden_part * scale_part * gain_two_f).astype(jnp.bfloat16))
    hidden_mid = jnp.concatenate(hidden_parts, axis=0)
    scale_two = jnp.concatenate(scale_parts, axis=0)
    normed_two = jnp.concatenate(normed_parts, axis=0)
    if parts == 2:
        sequence = jnp.concatenate(
            normed_parts + [swap(part, "tensor") for part in normed_parts], axis=0
        )
        token_rows = jnp.concatenate([sequence, swap(sequence, "core")], axis=0)
    else:
        token_rows = gather_rows(normed_two)
    logits = jnp.dot(token_rows, router_w, preferred_element_type=jnp.float32)
    gates = dense_gates(logits, routes_rows)

    mixture, rows_grad, gate_grads, expert_sums = 0.0, 0.0, [], []
    for g in range(groups):
        token_rows_g, cot_rows_g = token_rows, cot_rows
        if g > 0:
            run_hops(expert_sums, g - 1)
            token_rows_g, cot_rows_g, mixture, rows_grad, grads, gathered[g] = tie(
                (token_rows, cot_rows, mixture, rows_grad, grads, gathered[g]),
                [expert_sums[done] for done, _ in HOPS[g - 1]],
            )
            expert_sums.append(scatter_experts(grads, g - 1, starts))
        by_core = gathered[g].reshape(3, each, -1, 2, shard, D)
        group_gates = gates[:, g * each : (g + 1) * each]
        if shard == 16 and by_core.shape[2] == 8:
            mixture, rows_grad, gate_grad, grads = expert_call(
                token_rows_g,
                cot_rows_g,
                group_gates,
                by_core,
                (mixture, rows_grad) if g > 0 else None,
            )
        else:
            by_core = lax.dynamic_index_in_dim(by_core, lax.axis_index("core"), 3, keepdims=False)
            gate_w, up_w, down_w = by_core.reshape(3, each, -1, D)
            mix, rows, gate_grad, grads = expert_group(
                token_rows_g, cot_rows_g, group_gates, gate_w, up_w, down_w
            )
            mixture, rows_grad = mixture + mix, rows_grad + rows
        gate_grads.append(gate_grad)
    run_hops(expert_sums, groups - 1)
    mixture, rows_grad, grads = tie(
        (mixture, rows_grad, grads), [expert_sums[done] for done, _ in HOPS[groups - 1]]
    )
    expert_sums.append(scatter_experts(grads, groups - 1, starts))
    gate_grad_own = scatter_rows(jnp.concatenate(gate_grads, axis=1))
    if parts == 2:
        probs_own = gates[:own_rows]
    else:
        probs_own = lax.dynamic_slice_in_dim(
            gates, lax.axis_index("tensor") * own_rows, own_rows, 0
        )
    logit_grad = (
        probs_own * (gate_grad_own - jnp.sum(probs_own * gate_grad_own, axis=-1, keepdims=True))
    ).astype(jnp.bfloat16)
    router_part = lax.dot_general(
        logit_grad, router_w, contract_last, preferred_element_type=jnp.float32
    )
    router_grad = lax.dot_general(
        normed_two,
        jnp.pad(logit_grad, ((0, 0), (0, 128 - E))),
        contract_first,
        preferred_element_type=jnp.float32,
    )
    half_rows = seq_len
    mine = rows_grad[:half_rows] + swap(
        rows_grad[half_rows:].astype(jnp.bfloat16), "core"
    ).astype(jnp.float32)
    mid_parts, gain_two_grad = [], 0.0
    for c in range(chunks):
        part = slice(c * piece, (c + 1) * piece)
        if parts == 2:
            given = mine[own_rows + c * piece : own_rows + (c + 1) * piece]
            summed = mine[part] + swap(given.astype(jnp.bfloat16), "tensor").astype(jnp.float32)
        else:
            summed = scatter_tensor(mine.astype(jnp.bfloat16), False)
        mid_part, gain_part = norm_backward(
            hidden_mid[part], scale_two[part], gain_two_f, summed + router_part[part]
        )
        mid_parts.append(cotangent[part].astype(jnp.float32) + mid_part)
        gain_two_grad = gain_two_grad + gain_part
    mid_grad = jnp.concatenate(mid_parts, axis=0)
    if parts == 2:
        own_low = [part.astype(jnp.bfloat16) for part in mid_parts]
        other = jnp.concatenate([swap(part, "tensor") for part in own_low], axis=0)
        own_low = jnp.concatenate(own_low, axis=0)
        first = lax.axis_index("tensor") == 0
        mid_all = jnp.concatenate(
            [jnp.where(first, own_low, other), jnp.where(first, other, own_low)], axis=0
        )
    else:
        mid_all = gather_ordered(mid_grad.astype(jnp.bfloat16))
    run_hops(expert_sums, groups)
    mid_all, mixture = tie((mid_all, mixture), expert_sums)
    outputs = (hidden_mid + scatter_rows(mixture)).astype(jnp.bfloat16)
    out_wt_grad = lax.dot_general(
        mid_all, attn_out, contract_first, preferred_element_type=jnp.float32
    )
    column = jnp.arange(128, dtype=jnp.int32)[None, :]
    early = jnp.concatenate(
        [
            out_wt_grad.astype(jnp.bfloat16),
            jnp.where(column == E + 1, gain_two_grad[:, None], router_grad).astype(jnp.bfloat16),
        ],
        axis=1,
    )
    early = lax.psum_scatter(early, ("chip", "core"), scatter_dimension=0, tiled=True).astype(
        jnp.float32
    )
    attn_out_grad = jnp.dot(mid_all, out_wt, preferred_element_type=jnp.float32).astype(
        jnp.bfloat16
    )
    query_grad, key_grad, value_grad = attention_backward(
        query_rot, key_rot, value_hd, log_total, attn_out_grad
    )
    run_hops(expert_sums, groups + 1)
    query_grad, key_grad, value_grad = tie((query_grad, key_grad, value_grad), expert_sums)
    query_pg = unrotate(query_grad, cosine, sine).reshape(seq_len, -1).astype(jnp.bfloat16)
    key_pg = unrotate(key_grad, cosine, sine).reshape(seq_len, -1).astype(jnp.bfloat16)
    value_pg = value_grad.reshape(seq_len, -1).astype(jnp.bfloat16)
    proj_pg = jnp.concatenate([query_pg, key_pg, value_pg], axis=1)
    proj_w_grad = lax.dot_general(
        normed_all, proj_pg, contract_first, preferred_element_type=jnp.float32
    )
    normed_one_grad = scatter_tensor(
        lax.dot_general(
            proj_pg, proj_w, contract_last, preferred_element_type=jnp.float32
        ).astype(jnp.bfloat16),
        True,
    )
    input_part, gain_one_grad = norm_backward(inputs_f, scale_one, gain_one_f, normed_one_grad)
    input_grad = mid_grad + input_part
    late = jnp.concatenate(
        [
            proj_w_grad.astype(jnp.bfloat16),
            jnp.where(column == E, gain_one_grad[:, None], 0.0).astype(jnp.bfloat16),
        ],
        axis=1,
    )
    run_hops(expert_sums, groups + 2)
    late = tie(late, expert_sums)
    late = lax.psum_scatter(late, ("chip", "core"), scatter_dimension=0, tiled=True).astype(
        jnp.float32
    )
    run_hops(expert_sums, groups + 3)
    shared = early[:, q_cols:] + late[:, proj_cols:]
    if parts == 2:
        shared = shared + swap(shared, "tensor")
    else:
        shared = lax.psum(shared, "tensor")
    expert_grads = jnp.concatenate([each.result() for each in expert_sums], axis=1)
    expert_grads = expert_grads.reshape(3, E, shard * D)
    return (
        outputs,
        input_grad,
        shared[:, E],
        late[:, :q_cols],
        late[:, q_cols : q_cols + k_cols],
        late[:, q_cols + k_cols : proj_cols],
        early[:, :q_cols].T,
        shared[:, E + 1],
        shared[:, :E],
        expert_grads[0],
        expert_grads[1],
        expert_grads[2],
    )


def solution(mesh):
    dp, parts = mesh.devices.shape
    cores = jax.sharding.Mesh(mesh.devices.reshape(dp // 2, 2, parts), ("chip", "core", "tensor"))
    dp = ("chip", "core")
    every = ("chip", "core", "tensor")
    in_specs = (
        P(every, None),
        P(dp),
        P(dp, "tensor"),
        P(dp, "tensor"),
        P(dp, "tensor"),
        P("tensor", dp),
        P(dp),
        P(dp, None),
        P(None, every),
        P(None, every),
        P(None, every),
        P(dp, None),
        P(every, None),
    )
    out_specs = (
        P(every, None),
        P(every, None),
        P(dp),
        P(dp, "tensor"),
        P(dp, "tensor"),
        P(dp, "tensor"),
        P("tensor", dp),
        P(dp),
        P(dp, None),
        P(None, every),
        P(None, every),
        P(None, every),
    )

    return jax.shard_map(body, mesh=cores, in_specs=in_specs, out_specs=out_specs, check_vma=False)
```

```python
import functools

import jax
import jax.numpy as jnp
from jax import lax
from jax.experimental import pallas as pl
from jax.experimental.pallas import tpu as pltpu
from jax.sharding import PartitionSpec as P


D = 1536
HD = 64
E = 40
GROUPS = 5
RINGED = 5
TILES = 4
HOPS = (
    (),
    (),
    (),
    (),
    ((0, 1), (1, 1), (2, 1)),
    ((0, 1), (1, 1), (2, 1), (3, 1), (4, 1)),
    ((0, 1), (1, 1), (2, 1), (3, 1), (4, 1)),
    ((0, 1), (1, 1), (3, 1)),
    ((2, 1), (3, 1), (4, 2)),
)
BLOCK = 256
RING = (0, 2, 4, 6, 7, 5, 3, 1)


epsilon = 1e-06
contract_last = (((1,), (1,)), ((), ()))
contract_first = (((0,), (0,)), ((), ()))


def rope_tables(seq_len, width):
    position = jnp.arange(seq_len).astype(jnp.float32)
    freq = 10000.0 ** (-jnp.arange(width // 2).astype(jnp.float32) * 2.0 / width)
    angle = position[:, None] * freq[None, :]
    return (jnp.cos(angle)[:, None, :], jnp.sin(angle)[:, None, :])


def rotate(values, cosine, sine):
    half = values.shape[-1] // 2
    first_half = values[..., :half]
    second_half = values[..., half:]
    return jnp.concatenate(
        [first_half * cosine - second_half * sine, second_half * cosine + first_half * sine],
        axis=-1,
    )


def unrotate(grads, cosine, sine):
    half = grads.shape[-1] // 2
    first_half = grads[..., :half]
    second_half = grads[..., half:]
    return jnp.concatenate(
        [first_half * cosine + second_half * sine, second_half * cosine - first_half * sine],
        axis=-1,
    )


def rms_factor(values):
    return lax.rsqrt(jnp.mean(values * values, axis=-1, keepdims=True) + epsilon)


def norm_backward(values, factor, gain_f, normed_grad):
    weighted = normed_grad * gain_f
    values_grad = factor * weighted - values * factor**3 * jnp.mean(
        values * weighted, axis=-1, keepdims=True
    )
    return (values_grad, jnp.sum(normed_grad * values * factor, axis=0))


def block_scores(query_blk, key_rot, offset):
    rows, keys = query_blk.shape[0], key_rot.shape[0]
    scores = jnp.einsum(
        "qcgd,kcd->cgqk", query_blk, key_rot, preferred_element_type=jnp.float32
    ) * HD ** (-0.5)
    causal = (offset + jnp.arange(rows, dtype=jnp.int32))[:, None] >= jnp.arange(
        keys, dtype=jnp.int32
    )[None, :]
    return jnp.where(causal, scores, -1e30)


def attention_forward(query_rot, key_rot, value_hd):
    seq_len, heads, width = query_rot.shape
    kv_heads = key_rot.shape[1]
    block_rows = min(BLOCK, seq_len)
    grouped = query_rot.reshape(seq_len, kv_heads, heads // kv_heads, width)
    blocks = seq_len // block_rows
    half = max(1, blocks // 2)
    outs, logs = [None] * blocks, [None] * blocks
    for number in [block for first in range(half) for block in range(first, blocks, half)]:
        start, stop = number * block_rows, (number + 1) * block_rows
        scores = block_scores(grouped[start:stop], key_rot[:stop], start)
        highest_score = jnp.max(scores, axis=-1, keepdims=True)
        expo = jnp.exp(scores - highest_score)
        total = jnp.sum(expo, axis=-1, keepdims=True)
        prob_low = (expo / total).astype(jnp.bfloat16)
        attn_blk = jnp.einsum(
            "cgqk,kcd->qcgd", prob_low, value_hd[:stop], preferred_element_type=jnp.float32
        )
        outs[number] = attn_blk.astype(jnp.bfloat16).reshape(block_rows, heads * width)
        logs[number] = (highest_score + jnp.log(total))[..., 0]
        if number == blocks - half and half > 1:
            key_rot, value_hd, outs[0], outs[number] = lax.optimization_barrier(
                (key_rot, value_hd, outs[0], outs[number])
            )
    return outs, logs


def attention_backward(query_rot, key_rot, value_hd, logs, out_grad_all):
    seq_len, heads, width = query_rot.shape
    kv_heads = key_rot.shape[1]
    block_rows = min(BLOCK, seq_len)
    grouped = query_rot.reshape(seq_len, kv_heads, heads // kv_heads, width)
    grad_groups = out_grad_all.reshape(grouped.shape)
    query_grads = []
    key_acc = jnp.zeros((seq_len, kv_heads, width), jnp.float32)
    value_acc = key_acc
    for number, start in enumerate(range(0, seq_len, block_rows)):
        stop = start + block_rows
        query_blk, grad_blk = grouped[start:stop], grad_groups[start:stop]
        keys, values = key_rot[:stop], value_hd[:stop]
        scores = block_scores(query_blk, keys, start)
        attn_prob = jnp.exp(scores - logs[number][..., None])
        prob_low = attn_prob.astype(jnp.bfloat16)
        prob_grad = jnp.einsum(
            "qcgd,kcd->cgqk", grad_blk, values, preferred_element_type=jnp.float32
        )
        score_grad = (
            attn_prob * (prob_grad - jnp.sum(attn_prob * prob_grad, axis=-1, keepdims=True))
        ).astype(jnp.bfloat16)
        query_grad = jnp.einsum(
            "cgqk,kcd->qcgd", score_grad, keys, preferred_element_type=jnp.float32
        ) * HD ** (-0.5)
        key_part = jnp.einsum(
            "cgqk,qcgd->kcd", score_grad, query_blk, preferred_element_type=jnp.float32
        ) * HD ** (-0.5)
        value_part = jnp.einsum(
            "cgqk,qcgd->kcd", prob_low, grad_blk, preferred_element_type=jnp.float32
        )
        rest = ((0, seq_len - stop), (0, 0), (0, 0))
        key_acc = key_acc + jnp.pad(key_part, rest)
        value_acc = value_acc + jnp.pad(value_part, rest)
        query_grads.append(query_grad.reshape(block_rows, heads, width))
    return jnp.concatenate(query_grads, axis=0), key_acc, value_acc


def swap(values, axis):
    return lax.ppermute(values, axis, [(0, 1), (1, 0)])


def gather_ordered(values):
    if lax.axis_size("tensor") != 2:
        return lax.all_gather(values, "tensor", axis=0, tiled=True)
    other = swap(values, "tensor")
    first = lax.axis_index("tensor") == 0
    return jnp.concatenate(
        [jnp.where(first, values, other), jnp.where(first, other, values)], axis=0
    )


def gather_rows(values):
    if lax.axis_size("tensor") == 2:
        sequence = jnp.concatenate([values, swap(values, "tensor")], axis=0)
    else:
        sequence = lax.all_gather(values, "tensor", axis=0, tiled=True)
    return jnp.concatenate([sequence, swap(sequence, "core")], axis=0)


def scatter_tensor(values, ordered):
    if lax.axis_size("tensor") != 2:
        return lax.psum_scatter(values, "tensor", scatter_dimension=0, tiled=True).astype(
            jnp.float32
        )
    half = values.shape[0] // 2
    if ordered:
        first = lax.axis_index("tensor") == 0
        low, high = values[:half], values[half:]
        kept, given = jnp.where(first, low, high), jnp.where(first, high, low)
    else:
        kept, given = values[:half], values[half:]
    return kept.astype(jnp.float32) + swap(given, "tensor").astype(jnp.float32)


def scatter_rows(values):
    half = values.shape[0] // 2
    mine = values[:half].astype(jnp.float32) + swap(
        values[half:].astype(jnp.bfloat16), "core"
    ).astype(jnp.float32)
    return scatter_tensor(mine.astype(jnp.bfloat16), False)


def sequence_routes(routes, own_rows):
    if lax.axis_size("tensor") == 2:
        second = lax.axis_index("tensor") == 1
        low, high = routes[:own_rows], routes[own_rows:]
        routes = jnp.concatenate(
            [jnp.where(second, high, low), jnp.where(second, low, high)], axis=0
        )
    return jnp.concatenate([routes, swap(routes, "core")], axis=0)


def dense_gates(logits, routes):
    experts = jnp.arange(E, dtype=jnp.int32)
    used = jnp.any(routes[:, :, None] == experts[None, None, :], axis=1)
    top = jnp.max(jnp.where(used, logits, -jnp.inf), axis=-1, keepdims=True)
    expo = jnp.where(used, jnp.exp(jnp.minimum(logits - top, 0.0)), 0.0)
    return expo / jnp.sum(expo, axis=-1, keepdims=True)


class Ring:
    def __init__(self, grads, flip, starts):
        self.grads, self.step, self.hop_number = grads, -1 if flip else 1, 0
        self.count = len(RING)
        self.starts = starts
        far = self.count // 2
        self.state = (self.own(self.step * far), self.own(-self.step * (far - 1)))

    def own(self, ahead):
        start = self.starts[ahead % self.count]
        return lax.dynamic_index_in_dim(self.grads, start, 0, keepdims=False)

    def send(self, block, way):
        pairs = [(RING[i], RING[(i + way) % self.count]) for i in range(self.count)]
        return lax.ppermute(block, "chip", pairs)

    def hop(self):
        self.hop_number += 1
        hop, far = self.hop_number, self.count // 2
        ahead, behind = self.state
        ahead = self.send(ahead, self.step)
        if hop < far:
            ahead = self.add(ahead, self.own(self.step * (far - hop)))
        if hop < far - 1:
            behind = self.add(
                self.send(behind, -self.step), self.own(-self.step * (far - 1 - hop))
            )
        elif hop == far - 1:
            behind = self.send(behind, -self.step)
        self.state = (ahead, behind)

    def add(self, block, own):
        return (block.astype(jnp.float32) + own.astype(jnp.float32)).astype(jnp.bfloat16)

    def result(self):
        ahead, behind = self.state
        return (
            self.own(0).astype(jnp.float32)
            + ahead.astype(jnp.float32)
            + behind.astype(jnp.float32)
        )


class Whole:
    def __init__(self, grads):
        self.state = lax.psum_scatter(grads, "chip", scatter_dimension=0, tiled=True)[0]

    def hop(self):
        pass

    def result(self):
        return self.state.astype(jnp.float32)


def ring_chips():
    count = len(RING)
    if lax.axis_size("chip") != count:
        return None
    table = [[RING[(RING.index(c) + a) % count] for a in range(count)] for c in range(count)]
    mine = jnp.asarray(table, jnp.int32)[lax.axis_index("chip")]
    return [mine[a] for a in range(count)]


def scatter_experts(grads, number, starts):
    if number < RINGED and starts is not None:
        return Ring(grads, number % 2 == 1, starts)
    return Whole(grads)


def run_hops(sums, stage):
    for which, count in HOPS[stage]:
        for _ in range(count):
            sums[which].hop()


def tie(values, sums):
    values, states = lax.optimization_barrier((values, [each.state for each in sums]))
    for each, state in zip(sums, states):
        each.state = state
    return values


def expert_kernel(first, core_ref, tokens_ref, cot_ref, gates_ref, weights_ref, *refs):
    if not first:
        mix_in, rows_in, *refs = refs
    mix_out, rows_out, gate_grad_ref, grads_ref, mix, rows, sums, in_sem, out_sem = refs
    step, steps = pl.program_id(0), pl.num_programs(0)
    size = tokens_ref.shape[0] // TILES
    width = tokens_ref.shape[1]
    gate_w, up_w, down_w = (weights_ref[k].reshape(-1, width) for k in range(3))
    pair = gate_w.shape[0]

    def arriving(tile, which):
        part = pl.ds(tile * size, size)
        source, target = ((mix_in, mix), (rows_in, rows))[which]
        return pltpu.make_async_copy(source.at[part], target.at[part], in_sem.at[which, tile])

    def leaving(tile, which):
        part = pl.ds(tile * size, size)
        source, target = ((mix, mix_out), (rows, rows_out))[which]
        return pltpu.make_async_copy(source.at[part], target.at[part], out_sem.at[which, tile])

    def dot(left, right, contract):
        return lax.dot_general(
            left, right, (contract, ((), ())), preferred_element_type=jnp.float32
        )

    if not first:

        @pl.when(step == 0)
        def _():
            for tile in range(TILES):
                arriving(tile, 0).start()
                arriving(tile, 1).start()

    sums[...] = jnp.zeros_like(sums)

    def one_tile(tile, carry):
        part = pl.ds(pl.multiple_of(tile * size, size), size)
        tokens, cot = tokens_ref[part, :], cot_ref[part, :]
        gate_h = dot(gate_w, tokens, ((1,), (1,)))
        up_h = dot(up_w, tokens, ((1,), (1,)))
        cot_h = dot(down_w, cot, ((1,), (1,)))
        gates = jnp.broadcast_to(
            gates_ref[0, :, part][:, None, :], (2, pair // 2, size)
        ).reshape(pair, size)
        sigma = jax.nn.sigmoid(gate_h)
        silu = gate_h * sigma
        hidden_h = silu * up_h
        gate_grad_ref[0, :, part] = jnp.sum((hidden_h * cot_h).reshape(2, pair // 2, size), axis=1)
        weighted = (gates * hidden_h).astype(jnp.bfloat16)
        hidden_grad = gates * cot_h
        gate_hg = (hidden_grad * up_h * (sigma + silu * (1.0 - sigma))).astype(jnp.bfloat16)
        up_hg = (hidden_grad * silu).astype(jnp.bfloat16)

        @pl.when(step == 0)
        def _():
            if first:
                mix[part, :] = jnp.zeros((size, width), jnp.float32)
                rows[part, :] = jnp.zeros((size, width), jnp.float32)
            else:
                arriving(tile, 0).wait()
                arriving(tile, 1).wait()

        mix[part, :] += dot(weighted, down_w, ((0,), (0,)))
        rows[part, :] += dot(gate_hg, gate_w, ((0,), (0,))) + dot(up_hg, up_w, ((0,), (0,)))
        sums[0] += dot(gate_hg, tokens, ((1,), (0,)))
        sums[1] += dot(up_hg, tokens, ((1,), (0,)))
        sums[2] += dot(weighted, cot, ((1,), (0,)))

        @pl.when(step == steps - 1)
        def _():
            leaving(tile, 0).start()
            leaving(tile, 1).start()

        return carry

    lax.fori_loop(0, TILES, one_tile, 0)
    chips, _, _, shard, _ = grads_ref.shape
    grads = sums[...].astype(jnp.bfloat16).reshape(3, 2, chips, shard, width)
    for chip in range(chips):
        grads_ref[chip] = grads[:, :, chip]

    @pl.when(step == steps - 1)
    def _():
        for tile in range(TILES):
            leaving(tile, 0).wait()
            leaving(tile, 1).wait()


def expert_call(tokens, cot, gates, gathered, totals):
    first = totals is None
    count, width = tokens.shape
    _, each, chips, _, shard, _ = gathered.shape
    pair = 2 * chips * shard
    core = lax.axis_index("core").astype(jnp.int32)[None]
    gates = gates.T.reshape(each // 2, 2, count)
    whole = pl.BlockSpec((count, width), lambda i, core: (0, 0), pipeline_mode=pl.Buffered(1))
    by_pair = pl.BlockSpec((1, 2, count), lambda i, core: (i, 0, 0))
    anywhere = pl.BlockSpec(memory_space=pl.ANY)
    total = jax.ShapeDtypeStruct((count, width), jnp.float32)
    mix, rows, gate_grad, grads = pl.pallas_call(
        functools.partial(expert_kernel, first),
        grid_spec=pltpu.PrefetchScalarGridSpec(
            num_scalar_prefetch=1,
            grid=(each // 2,),
            in_specs=[
                whole,
                whole,
                by_pair,
                pl.BlockSpec(
                    (3, 2, chips, None, shard, width), lambda i, core: (0, i, 0, core[0], 0, 0)
                ),
            ]
            + ([] if first else [anywhere, anywhere]),
            out_specs=[
                anywhere,
                anywhere,
                by_pair,
                pl.BlockSpec((chips, 3, 2, shard, width), lambda i, core: (0, 0, i, 0, 0)),
            ],
            scratch_shapes=[
                pltpu.VMEM((count, width), jnp.float32),
                pltpu.VMEM((count, width), jnp.float32),
                pltpu.VMEM((3, pair, width), jnp.float32),
                pltpu.SemaphoreType.DMA((2, TILES)),
                pltpu.SemaphoreType.DMA((2, TILES)),
            ],
        ),
        out_shape=[
            total,
            total,
            jax.ShapeDtypeStruct(gates.shape, jnp.float32),
            jax.ShapeDtypeStruct((chips, 3, each, shard, width), jnp.bfloat16),
        ],
        input_output_aliases={} if first else {5: 0, 6: 1},
        compiler_params=pltpu.CompilerParams(vmem_limit_bytes=67043328),
        cost_estimate=pl.CostEstimate(
            flops=9 * count * width * pair * each,
            bytes_accessed=4 * 4 * count * width + 12 * each * chips * shard * width,
            transcendentals=count * pair * each // 2,
        ),
        name="experts",
    )(core, tokens, cot, gates, gathered, *(() if first else totals))
    return mix, rows, gate_grad.reshape(each, count).T, grads


def expert_group(tokens, cot, gates, gate_w, up_w, down_w):
    rows = tokens.shape[0]
    count, hidden = gate_w.shape[:2]
    flat = (count * hidden, D)
    gate_w, up_w, down_w = gate_w.reshape(flat), up_w.reshape(flat), down_w.reshape(flat)
    wide = jnp.broadcast_to(gates[:, :, None], (rows, count, hidden)).reshape(rows, -1)
    gate_h = lax.dot_general(tokens, gate_w, contract_last, preferred_element_type=jnp.float32)
    up_h = lax.dot_general(tokens, up_w, contract_last, preferred_element_type=jnp.float32)
    cot_h = lax.dot_general(cot, down_w, contract_last, preferred_element_type=jnp.float32)
    sigma = jax.nn.sigmoid(gate_h)
    silu = gate_h * sigma
    hidden_h = silu * up_h
    gate_grad = jnp.sum((hidden_h * cot_h).reshape(rows, count, hidden), axis=-1)
    hidden_grad = wide * cot_h
    weighted = (wide * hidden_h).astype(jnp.bfloat16)
    gate_hg = (hidden_grad * up_h * sigma * (1.0 + gate_h * (1.0 - sigma))).astype(jnp.bfloat16)
    up_hg = (hidden_grad * silu).astype(jnp.bfloat16)
    mixture = jnp.dot(weighted, down_w, preferred_element_type=jnp.float32)
    rows_grad = jnp.dot(gate_hg, gate_w, preferred_element_type=jnp.float32) + jnp.dot(
        up_hg, up_w, preferred_element_type=jnp.float32
    )
    grads = jnp.stack([
        lax.dot_general(left, right, contract_first, preferred_element_type=jnp.float32)
        .astype(jnp.bfloat16)
        .reshape(count, hidden, D)
        for left, right in ((gate_hg, tokens), (up_hg, tokens), (weighted, cot))
    ])
    return mixture, rows_grad, gate_grad, grads


def body(
    inputs,
    gain_attn,
    w_query,
    w_key,
    w_value,
    w_out,
    gain_moe,
    w_router,
    w_gate,
    w_up,
    w_down,
    routes,
    cotangent,
):
    parts = lax.axis_size("tensor")
    own_rows = inputs.shape[0]
    seq_len = own_rows * parts
    cosine, sine = rope_tables(seq_len, HD)
    inputs_f = inputs.astype(jnp.float32)
    q_cols, k_cols = w_query.shape[1], w_key.shape[1]
    proj_cols = q_cols + 2 * k_cols
    filler = jnp.zeros((w_query.shape[0], 126 - E), jnp.bfloat16)
    packed = jnp.concatenate(
        [w_query, w_key, w_value, w_out.T, w_router, gain_attn[:, None], gain_moe[:, None], filler],
        axis=1,
    )
    packed = lax.all_gather(packed, ("chip", "core"), axis=0, tiled=True)
    proj_w, out_wt, small = jnp.split(packed, [proj_cols, proj_cols + q_cols], axis=1)
    query_w, key_w, value_w = jnp.split(proj_w, [q_cols, q_cols + k_cols], axis=1)
    router_w = small[:, :E]
    gain_one_f = small[:, E].astype(jnp.float32)
    gain_two_f = small[:, E + 1].astype(jnp.float32)

    shard = w_gate.shape[1] // D
    starts = ring_chips()
    groups = GROUPS
    each = E // groups
    stacked = [w.reshape(E, shard, D) for w in (w_gate, w_up, w_down)]
    gathered = []
    for g in range(groups):
        part = jnp.stack([w[g * each : (g + 1) * each] for w in stacked])
        gathered.append(lax.all_gather(part, ("chip", "core"), axis=2, tiled=True))

    inputs_all = gather_ordered(inputs)
    inputs_all, cot_later = lax.optimization_barrier((inputs_all, cotangent))
    cot_rows = gather_rows(cot_later)
    routes_rows = sequence_routes(routes, own_rows)

    scale_one = rms_factor(inputs_f)
    inputs_all = inputs_all.astype(jnp.float32)
    normed_all = (inputs_all * rms_factor(inputs_all) * gain_one_f).astype(jnp.bfloat16)
    query_proj = jnp.dot(normed_all, query_w, preferred_element_type=jnp.float32)
    key_proj = jnp.dot(normed_all, key_w, preferred_element_type=jnp.float32)
    value_proj = jnp.dot(normed_all, value_w, preferred_element_type=jnp.float32)
    query_rot = rotate(query_proj.reshape(seq_len, -1, HD), cosine, sine).astype(jnp.bfloat16)
    key_rot = rotate(key_proj.reshape(seq_len, -1, HD), cosine, sine).astype(jnp.bfloat16)
    value_hd = value_proj.reshape(seq_len, -1, HD).astype(jnp.bfloat16)
    attn_outs, log_total = attention_forward(query_rot, key_rot, value_hd)
    attn_out = jnp.concatenate(attn_outs, axis=0)
    chunks = len(attn_outs) // 2 if parts == 2 else 1
    piece = own_rows // chunks
    hidden_parts, scale_parts, normed_parts = [], [], []
    for c in range(chunks):
        both = jnp.concatenate([attn_outs[c], attn_outs[c + chunks]], axis=0) if parts == 2 else attn_out
        hidden_part = inputs_f[c * piece : (c + 1) * piece] + scatter_tensor(
            lax.dot_general(
                both, out_wt, contract_last, preferred_element_type=jnp.float32
            ).astype(jnp.bfloat16),
            True,
        )
        scale_part = rms_factor(hidden_part)
        hidden_parts.append(hidden_part)
        scale_parts.append(scale_part)
        normed_parts.append((hidden_part * scale_part * gain_two_f).astype(jnp.bfloat16))
    hidden_mid = jnp.concatenate(hidden_parts, axis=0)
    scale_two = jnp.concatenate(scale_parts, axis=0)
    normed_two = jnp.concatenate(normed_parts, axis=0)
    if parts == 2:
        sequence = jnp.concatenate(
            normed_parts + [swap(part, "tensor") for part in normed_parts], axis=0
        )
        token_rows = jnp.concatenate([sequence, swap(sequence, "core")], axis=0)
    else:
        token_rows = gather_rows(normed_two)
    logits = jnp.dot(token_rows, router_w, preferred_element_type=jnp.float32)
    gates = dense_gates(logits, routes_rows)

    mixture, rows_grad, gate_grads, expert_sums = 0.0, 0.0, [], []
    for g in range(groups):
        token_rows_g, cot_rows_g = token_rows, cot_rows
        if g > 0:
            run_hops(expert_sums, g - 1)
            token_rows_g, cot_rows_g, mixture, rows_grad, grads, gathered[g] = tie(
                (token_rows, cot_rows, mixture, rows_grad, grads, gathered[g]),
                [expert_sums[done] for done, _ in HOPS[g - 1]],
            )
            expert_sums.append(scatter_experts(grads, g - 1, starts))
        by_core = gathered[g].reshape(3, each, -1, 2, shard, D)
        group_gates = gates[:, g * each : (g + 1) * each]
        if shard == 16 and by_core.shape[2] == 8:
            mixture, rows_grad, gate_grad, grads = expert_call(
                token_rows_g,
                cot_rows_g,
                group_gates,
                by_core,
                (mixture, rows_grad) if g > 0 else None,
            )
        else:
            by_core = lax.dynamic_index_in_dim(by_core, lax.axis_index("core"), 3, keepdims=False)
            gate_w, up_w, down_w = by_core.reshape(3, each, -1, D)
            mix, rows, gate_grad, grads = expert_group(
                token_rows_g, cot_rows_g, group_gates, gate_w, up_w, down_w
            )
            mixture, rows_grad = mixture + mix, rows_grad + rows
            grads = jnp.moveaxis(grads.reshape(3, each, -1, shard, D), 2, 0)
        gate_grads.append(gate_grad)
    run_hops(expert_sums, groups - 1)
    mixture, rows_grad, grads = tie(
        (mixture, rows_grad, grads), [expert_sums[done] for done, _ in HOPS[groups - 1]]
    )
    expert_sums.append(scatter_experts(grads, groups - 1, starts))
    gate_grad_own = scatter_rows(jnp.concatenate(gate_grads, axis=1))
    if parts == 2:
        probs_own = gates[:own_rows]
    else:
        probs_own = lax.dynamic_slice_in_dim(
            gates, lax.axis_index("tensor") * own_rows, own_rows, 0
        )
    logit_grad = (
        probs_own * (gate_grad_own - jnp.sum(probs_own * gate_grad_own, axis=-1, keepdims=True))
    ).astype(jnp.bfloat16)
    router_part = lax.dot_general(
        logit_grad, router_w, contract_last, preferred_element_type=jnp.float32
    )
    router_grad = lax.dot_general(
        normed_two,
        jnp.pad(logit_grad, ((0, 0), (0, 128 - E))),
        contract_first,
        preferred_element_type=jnp.float32,
    )
    half_rows = seq_len
    theirs = rows_grad[half_rows:].astype(jnp.bfloat16)
    mine = rows_grad[:half_rows] + swap(theirs, "core").astype(jnp.float32)
    mid_parts, gain_two_grad = [], 0.0
    for c in range(chunks):
        part = slice(c * piece, (c + 1) * piece)
        if parts == 2:
            given = mine[own_rows + c * piece : own_rows + (c + 1) * piece]
            summed = mine[part] + swap(given.astype(jnp.bfloat16), "tensor").astype(jnp.float32)
        else:
            summed = scatter_tensor(mine.astype(jnp.bfloat16), False)
        mid_part, gain_part = norm_backward(
            hidden_mid[part], scale_two[part], gain_two_f, summed + router_part[part]
        )
        mid_parts.append(cotangent[part].astype(jnp.float32) + mid_part)
        gain_two_grad = gain_two_grad + gain_part
    mid_grad = jnp.concatenate(mid_parts, axis=0)
    if parts == 2:
        own_low = [part.astype(jnp.bfloat16) for part in mid_parts]
        other = jnp.concatenate([swap(part, "tensor") for part in own_low], axis=0)
        own_low = jnp.concatenate(own_low, axis=0)
        first = lax.axis_index("tensor") == 0
        mid_all = jnp.concatenate(
            [jnp.where(first, own_low, other), jnp.where(first, other, own_low)], axis=0
        )
    else:
        mid_all = gather_ordered(mid_grad.astype(jnp.bfloat16))
    run_hops(expert_sums, groups)
    mid_all, mixture = tie((mid_all, mixture), expert_sums)
    mixed = swap(mixture[seq_len:].astype(jnp.bfloat16), "core")
    mixed = (mixture[:seq_len] + mixed.astype(jnp.float32)).astype(jnp.bfloat16)
    mixed = scatter_tensor(mixed, False)
    outputs = (hidden_mid + mixed).astype(jnp.bfloat16)
    out_wt_grad = lax.dot_general(
        mid_all, attn_out, contract_first, preferred_element_type=jnp.float32
    )
    column = jnp.arange(128, dtype=jnp.int32)[None, :]
    early = jnp.concatenate(
        [
            out_wt_grad.astype(jnp.bfloat16),
            jnp.where(column == E + 1, gain_two_grad[:, None], router_grad).astype(jnp.bfloat16),
        ],
        axis=1,
    )
    early = lax.psum_scatter(early, ("chip", "core"), scatter_dimension=0, tiled=True).astype(
        jnp.float32
    )
    attn_out_grad = jnp.dot(mid_all, out_wt, preferred_element_type=jnp.float32).astype(
        jnp.bfloat16
    )
    query_grad, key_grad, value_grad = attention_backward(
        query_rot, key_rot, value_hd, log_total, attn_out_grad
    )
    run_hops(expert_sums, groups + 1)
    query_grad, key_grad, value_grad = tie((query_grad, key_grad, value_grad), expert_sums)
    query_pg = unrotate(query_grad, cosine, sine).reshape(seq_len, -1).astype(jnp.bfloat16)
    key_pg = unrotate(key_grad, cosine, sine).reshape(seq_len, -1).astype(jnp.bfloat16)
    value_pg = value_grad.reshape(seq_len, -1).astype(jnp.bfloat16)
    proj_pg = jnp.concatenate([query_pg, key_pg, value_pg], axis=1)
    proj_w_grad = lax.dot_general(
        normed_all, proj_pg, contract_first, preferred_element_type=jnp.float32
    )
    summed = lax.dot_general(
        proj_pg, proj_w, contract_last, preferred_element_type=jnp.float32
    ).astype(jnp.bfloat16)
    normed_one_grad = scatter_tensor(summed, True)
    input_part, gain_one_grad = norm_backward(inputs_f, scale_one, gain_one_f, normed_one_grad)
    input_grad = mid_grad + input_part
    late = jnp.concatenate(
        [
            proj_w_grad.astype(jnp.bfloat16),
            jnp.where(column == E, gain_one_grad[:, None], 0.0).astype(jnp.bfloat16),
        ],
        axis=1,
    )
    run_hops(expert_sums, groups + 2)
    late = tie(late, expert_sums)
    late = lax.psum_scatter(late, ("chip", "core"), scatter_dimension=0, tiled=True).astype(
        jnp.float32
    )
    run_hops(expert_sums, groups + 3)
    shared = early[:, q_cols:] + late[:, proj_cols:]
    if parts == 2:
        shared = shared + swap(shared, "tensor")
    else:
        shared = lax.psum(shared, "tensor")
    pieces = [each_sum.result().reshape(3, each, shard * D) for each_sum in expert_sums]
    expert_grads = [jnp.concatenate([piece[k] for piece in pieces], axis=0) for k in range(3)]
    return (
        outputs,
        input_grad,
        shared[:, E],
        late[:, :q_cols],
        late[:, q_cols : q_cols + k_cols],
        late[:, q_cols + k_cols : proj_cols],
        early[:, :q_cols].T,
        shared[:, E + 1],
        shared[:, :E],
        expert_grads[0],
        expert_grads[1],
        expert_grads[2],
    )


def solution(mesh):
    dp, parts = mesh.devices.shape
    cores = jax.sharding.Mesh(mesh.devices.reshape(dp // 2, 2, parts), ("chip", "core", "tensor"))
    dp = ("chip", "core")
    every = ("chip", "core", "tensor")
    in_specs = (
        P(every, None),
        P(dp),
        P(dp, "tensor"),
        P(dp, "tensor"),
        P(dp, "tensor"),
        P("tensor", dp),
        P(dp),
        P(dp, None),
        P(None, every),
        P(None, every),
        P(None, every),
        P(dp, None),
        P(every, None),
    )
    out_specs = (
        P(every, None),
        P(every, None),
        P(dp),
        P(dp, "tensor"),
        P(dp, "tensor"),
        P(dp, "tensor"),
        P("tensor", dp),
        P(dp),
        P(dp, None),
        P(None, every),
        P(None, every),
        P(None, every),
    )

    return jax.shard_map(body, mesh=cores, in_specs=in_specs, out_specs=out_specs, check_vma=False)
```

```python
import functools

import jax
import jax.numpy as jnp
from jax import lax
from jax.experimental import pallas as pl
from jax.experimental.pallas import tpu as pltpu
from jax.sharding import PartitionSpec as P


D = 1536
HD = 64
E = 40
GROUPS = 5
RINGED = 5
TILES = 4
HOPS = (
    (),
    (),
    (),
    (),
    ((0, 1), (1, 1), (2, 1)),
    ((0, 1), (1, 1), (2, 1), (3, 1), (4, 1)),
    ((0, 1), (1, 1)),
    ((0, 1), (1, 1), (2, 1), (3, 1), (4, 1)),
    ((2, 1), (3, 1), (4, 1)),
    ((3, 1), (4, 1)),
)
BLOCK = 256
RING = (0, 2, 4, 6, 7, 5, 3, 1)


epsilon = 1e-06
contract_last = (((1,), (1,)), ((), ()))
contract_first = (((0,), (0,)), ((), ()))


def rope_tables(seq_len, width):
    position = jnp.arange(seq_len).astype(jnp.float32)
    freq = 10000.0 ** (-jnp.arange(width // 2).astype(jnp.float32) * 2.0 / width)
    angle = position[:, None] * freq[None, :]
    return (jnp.cos(angle)[:, None, :], jnp.sin(angle)[:, None, :])


def rotate(values, cosine, sine):
    half = values.shape[-1] // 2
    first_half = values[..., :half]
    second_half = values[..., half:]
    return jnp.concatenate(
        [first_half * cosine - second_half * sine, second_half * cosine + first_half * sine],
        axis=-1,
    )


def unrotate(grads, cosine, sine):
    half = grads.shape[-1] // 2
    first_half = grads[..., :half]
    second_half = grads[..., half:]
    return jnp.concatenate(
        [first_half * cosine + second_half * sine, second_half * cosine - first_half * sine],
        axis=-1,
    )


def rms_factor(values):
    return lax.rsqrt(jnp.mean(values * values, axis=-1, keepdims=True) + epsilon)


def norm_backward(values, factor, gain_f, normed_grad):
    weighted = normed_grad * gain_f
    values_grad = factor * weighted - values * factor**3 * jnp.mean(
        values * weighted, axis=-1, keepdims=True
    )
    return (values_grad, jnp.sum(normed_grad * values * factor, axis=0))


def block_scores(query_blk, key_rot, offset):
    rows, keys = query_blk.shape[0], key_rot.shape[0]
    scores = jnp.einsum(
        "qcgd,kcd->cgqk", query_blk, key_rot, preferred_element_type=jnp.float32
    ) * HD ** (-0.5)
    causal = (offset + jnp.arange(rows, dtype=jnp.int32))[:, None] >= jnp.arange(
        keys, dtype=jnp.int32
    )[None, :]
    return jnp.where(causal, scores, -1e30)


def attention_forward(query_rot, key_rot, value_hd):
    seq_len, heads, width = query_rot.shape
    kv_heads = key_rot.shape[1]
    block_rows = min(BLOCK, seq_len)
    grouped = query_rot.reshape(seq_len, kv_heads, heads // kv_heads, width)
    blocks = seq_len // block_rows
    half = max(1, blocks // 2)
    outs, logs = [None] * blocks, [None] * blocks
    for number in [block for first in range(half) for block in range(first, blocks, half)]:
        start, stop = number * block_rows, (number + 1) * block_rows
        scores = block_scores(grouped[start:stop], key_rot[:stop], start)
        highest_score = jnp.max(scores, axis=-1, keepdims=True)
        expo = jnp.exp(scores - highest_score)
        total = jnp.sum(expo, axis=-1, keepdims=True)
        prob_low = (expo / total).astype(jnp.bfloat16)
        attn_blk = jnp.einsum(
            "cgqk,kcd->qcgd", prob_low, value_hd[:stop], preferred_element_type=jnp.float32
        )
        outs[number] = attn_blk.astype(jnp.bfloat16).reshape(block_rows, heads * width)
        logs[number] = (highest_score + jnp.log(total))[..., 0]
        if number == blocks - half and half > 1:
            key_rot, value_hd, outs[0], outs[number] = lax.optimization_barrier(
                (key_rot, value_hd, outs[0], outs[number])
            )
    return outs, logs


def attention_backward(query_rot, key_rot, value_hd, logs, out_grad_all):
    seq_len, heads, width = query_rot.shape
    kv_heads = key_rot.shape[1]
    block_rows = min(BLOCK, seq_len)
    grouped = query_rot.reshape(seq_len, kv_heads, heads // kv_heads, width)
    grad_groups = out_grad_all.reshape(grouped.shape)
    query_grads = []
    key_acc = jnp.zeros((seq_len, kv_heads, width), jnp.float32)
    value_acc = key_acc
    for number, start in enumerate(range(0, seq_len, block_rows)):
        stop = start + block_rows
        query_blk, grad_blk = grouped[start:stop], grad_groups[start:stop]
        keys, values = key_rot[:stop], value_hd[:stop]
        scores = block_scores(query_blk, keys, start)
        attn_prob = jnp.exp(scores - logs[number][..., None])
        prob_low = attn_prob.astype(jnp.bfloat16)
        prob_grad = jnp.einsum(
            "qcgd,kcd->cgqk", grad_blk, values, preferred_element_type=jnp.float32
        )
        score_grad = (
            attn_prob * (prob_grad - jnp.sum(attn_prob * prob_grad, axis=-1, keepdims=True))
        ).astype(jnp.bfloat16)
        query_grad = jnp.einsum(
            "cgqk,kcd->qcgd", score_grad, keys, preferred_element_type=jnp.float32
        ) * HD ** (-0.5)
        key_part = jnp.einsum(
            "cgqk,qcgd->kcd", score_grad, query_blk, preferred_element_type=jnp.float32
        ) * HD ** (-0.5)
        value_part = jnp.einsum(
            "cgqk,qcgd->kcd", prob_low, grad_blk, preferred_element_type=jnp.float32
        )
        rest = ((0, seq_len - stop), (0, 0), (0, 0))
        key_acc = key_acc + jnp.pad(key_part, rest)
        value_acc = value_acc + jnp.pad(value_part, rest)
        query_grads.append(query_grad.reshape(block_rows, heads, width))
    return jnp.concatenate(query_grads, axis=0), key_acc, value_acc


def swap(values, axis):
    return lax.ppermute(values, axis, [(0, 1), (1, 0)])


def gather_ordered(values):
    if lax.axis_size("tensor") != 2:
        return lax.all_gather(values, "tensor", axis=0, tiled=True)
    other = swap(values, "tensor")
    first = lax.axis_index("tensor") == 0
    return jnp.concatenate(
        [jnp.where(first, values, other), jnp.where(first, other, values)], axis=0
    )


def gather_rows(values):
    if lax.axis_size("tensor") == 2:
        sequence = jnp.concatenate([values, swap(values, "tensor")], axis=0)
    else:
        sequence = lax.all_gather(values, "tensor", axis=0, tiled=True)
    return jnp.concatenate([sequence, swap(sequence, "core")], axis=0)


def scatter_tensor(values, ordered):
    if lax.axis_size("tensor") != 2:
        return lax.psum_scatter(values, "tensor", scatter_dimension=0, tiled=True).astype(
            jnp.float32
        )
    half = values.shape[0] // 2
    if ordered:
        first = lax.axis_index("tensor") == 0
        low, high = values[:half], values[half:]
        kept, given = jnp.where(first, low, high), jnp.where(first, high, low)
    else:
        kept, given = values[:half], values[half:]
    return kept.astype(jnp.float32) + swap(given, "tensor").astype(jnp.float32)


def scatter_rows(values):
    half = values.shape[0] // 2
    mine = values[:half].astype(jnp.float32) + swap(
        values[half:].astype(jnp.bfloat16), "core"
    ).astype(jnp.float32)
    return scatter_tensor(mine.astype(jnp.bfloat16), False)


def sequence_routes(routes, own_rows):
    if lax.axis_size("tensor") == 2:
        second = lax.axis_index("tensor") == 1
        low, high = routes[:own_rows], routes[own_rows:]
        routes = jnp.concatenate(
            [jnp.where(second, high, low), jnp.where(second, low, high)], axis=0
        )
    return jnp.concatenate([routes, swap(routes, "core")], axis=0)


def dense_gates(logits, routes):
    experts = jnp.arange(E, dtype=jnp.int32)
    used = jnp.any(routes[:, :, None] == experts[None, None, :], axis=1)
    top = jnp.max(jnp.where(used, logits, -jnp.inf), axis=-1, keepdims=True)
    expo = jnp.where(used, jnp.exp(jnp.minimum(logits - top, 0.0)), 0.0)
    return expo / jnp.sum(expo, axis=-1, keepdims=True)


class Ring:
    def __init__(self, grads, flip, starts):
        self.grads, self.step, self.hop_number = grads, -1 if flip else 1, 0
        self.count = len(RING)
        self.starts = starts
        far = self.count // 2
        self.state = (self.own(self.step * far), self.own(-self.step * (far - 1)))

    def own(self, ahead):
        start = self.starts[ahead % self.count]
        return lax.dynamic_index_in_dim(self.grads, start, 0, keepdims=False)

    def send(self, block, way):
        pairs = [(RING[i], RING[(i + way) % self.count]) for i in range(self.count)]
        return lax.ppermute(block, "chip", pairs)

    def hop(self):
        self.hop_number += 1
        hop, far = self.hop_number, self.count // 2
        ahead, behind = self.state
        ahead = self.send(ahead, self.step)
        if hop < far:
            ahead = self.add(ahead, self.own(self.step * (far - hop)))
        if hop < far - 1:
            behind = self.add(
                self.send(behind, -self.step), self.own(-self.step * (far - 1 - hop))
            )
        elif hop == far - 1:
            behind = self.send(behind, -self.step)
        self.state = (ahead, behind)

    def add(self, block, own):
        return (block.astype(jnp.float32) + own.astype(jnp.float32)).astype(jnp.bfloat16)

    def result(self):
        ahead, behind = self.state
        return (
            self.own(0).astype(jnp.float32)
            + ahead.astype(jnp.float32)
            + behind.astype(jnp.float32)
        )


class Whole:
    def __init__(self, grads):
        self.state = lax.psum_scatter(grads, "chip", scatter_dimension=0, tiled=True)[0]

    def hop(self):
        pass

    def result(self):
        return self.state.astype(jnp.float32)


def ring_chips():
    count = len(RING)
    if lax.axis_size("chip") != count:
        return None
    table = [[RING[(RING.index(c) + a) % count] for a in range(count)] for c in range(count)]
    mine = jnp.asarray(table, jnp.int32)[lax.axis_index("chip")]
    return [mine[a] for a in range(count)]


def scatter_experts(grads, number, starts):
    if number < RINGED and starts is not None:
        return Ring(grads, number % 2 == 1, starts)
    return Whole(grads)


def run_hops(sums, stage):
    for which, count in HOPS[stage]:
        for _ in range(count):
            sums[which].hop()


def tie(values, sums):
    values, states = lax.optimization_barrier((values, [each.state for each in sums]))
    for each, state in zip(sums, states):
        each.state = state
    return values


def expert_kernel(first, core_ref, tokens_ref, cot_ref, gates_ref, weights_ref, *refs):
    if not first:
        mix_in, rows_in, *refs = refs
    mix_out, rows_out, gate_grad_ref, grads_ref, mix, rows, sums, in_sem, out_sem = refs
    step, steps = pl.program_id(0), pl.num_programs(0)
    size = tokens_ref.shape[0] // TILES
    width = tokens_ref.shape[1]
    gate_w, up_w, down_w = (weights_ref[k].reshape(-1, width) for k in range(3))
    pair = gate_w.shape[0]

    def arriving(tile, which):
        part = pl.ds(tile * size, size)
        source, target = ((mix_in, mix), (rows_in, rows))[which]
        return pltpu.make_async_copy(source.at[part], target.at[part], in_sem.at[which, tile])

    def leaving(tile, which):
        part = pl.ds(tile * size, size)
        source, target = ((mix, mix_out), (rows, rows_out))[which]
        return pltpu.make_async_copy(source.at[part], target.at[part], out_sem.at[which, tile])

    def dot(left, right, contract):
        return lax.dot_general(
            left, right, (contract, ((), ())), preferred_element_type=jnp.float32
        )

    if not first:

        @pl.when(step == 0)
        def _():
            for tile in range(TILES):
                arriving(tile, 0).start()
                arriving(tile, 1).start()

    sums[...] = jnp.zeros_like(sums)

    def one_tile(tile, carry):
        part = pl.ds(pl.multiple_of(tile * size, size), size)
        tokens, cot = tokens_ref[part, :], cot_ref[part, :]
        gate_h = dot(gate_w, tokens, ((1,), (1,)))
        up_h = dot(up_w, tokens, ((1,), (1,)))
        cot_h = dot(down_w, cot, ((1,), (1,)))
        gates = jnp.broadcast_to(
            gates_ref[0, :, part][:, None, :], (2, pair // 2, size)
        ).reshape(pair, size)
        sigma = jax.nn.sigmoid(gate_h)
        silu = gate_h * sigma
        hidden_h = silu * up_h
        gate_grad_ref[0, :, part] = jnp.sum((hidden_h * cot_h).reshape(2, pair // 2, size), axis=1)
        weighted = (gates * hidden_h).astype(jnp.bfloat16)
        hidden_grad = gates * cot_h
        gate_hg = (hidden_grad * up_h * (sigma + silu * (1.0 - sigma))).astype(jnp.bfloat16)
        up_hg = (hidden_grad * silu).astype(jnp.bfloat16)

        @pl.when(step == 0)
        def _():
            if first:
                mix[part, :] = jnp.zeros((size, width), jnp.float32)
                rows[part, :] = jnp.zeros((size, width), jnp.float32)
            else:
                arriving(tile, 0).wait()
                arriving(tile, 1).wait()

        mix[part, :] += dot(weighted, down_w, ((0,), (0,)))
        rows[part, :] += dot(gate_hg, gate_w, ((0,), (0,))) + dot(up_hg, up_w, ((0,), (0,)))
        sums[0] += dot(gate_hg, tokens, ((1,), (0,)))
        sums[1] += dot(up_hg, tokens, ((1,), (0,)))
        sums[2] += dot(weighted, cot, ((1,), (0,)))

        @pl.when(step == steps - 1)
        def _():
            leaving(tile, 0).start()
            leaving(tile, 1).start()

        return carry

    lax.fori_loop(0, TILES, one_tile, 0)
    chips, _, _, shard, _ = grads_ref.shape
    grads = sums[...].astype(jnp.bfloat16).reshape(3, 2, chips, shard, width)
    for chip in range(chips):
        grads_ref[chip] = grads[:, :, chip]

    @pl.when(step == steps - 1)
    def _():
        for tile in range(TILES):
            leaving(tile, 0).wait()
            leaving(tile, 1).wait()


def expert_call(tokens, cot, gates, gathered, totals):
    first = totals is None
    count, width = tokens.shape
    _, each, chips, _, shard, _ = gathered.shape
    pair = 2 * chips * shard
    core = lax.axis_index("core").astype(jnp.int32)[None]
    gates = gates.T.reshape(each // 2, 2, count)
    whole = pl.BlockSpec((count, width), lambda i, core: (0, 0), pipeline_mode=pl.Buffered(1))
    by_pair = pl.BlockSpec((1, 2, count), lambda i, core: (i, 0, 0))
    anywhere = pl.BlockSpec(memory_space=pl.ANY)
    total = jax.ShapeDtypeStruct((count, width), jnp.float32)
    mix, rows, gate_grad, grads = pl.pallas_call(
        functools.partial(expert_kernel, first),
        grid_spec=pltpu.PrefetchScalarGridSpec(
            num_scalar_prefetch=1,
            grid=(each // 2,),
            in_specs=[
                whole,
                whole,
                by_pair,
                pl.BlockSpec(
                    (3, 2, chips, None, shard, width), lambda i, core: (0, i, 0, core[0], 0, 0)
                ),
            ]
            + ([] if first else [anywhere, anywhere]),
            out_specs=[
                anywhere,
                anywhere,
                by_pair,
                pl.BlockSpec((chips, 3, 2, shard, width), lambda i, core: (0, 0, i, 0, 0)),
            ],
            scratch_shapes=[
                pltpu.VMEM((count, width), jnp.float32),
                pltpu.VMEM((count, width), jnp.float32),
                pltpu.VMEM((3, pair, width), jnp.float32),
                pltpu.SemaphoreType.DMA((2, TILES)),
                pltpu.SemaphoreType.DMA((2, TILES)),
            ],
        ),
        out_shape=[
            total,
            total,
            jax.ShapeDtypeStruct(gates.shape, jnp.float32),
            jax.ShapeDtypeStruct((chips, 3, each, shard, width), jnp.bfloat16),
        ],
        input_output_aliases={} if first else {5: 0, 6: 1},
        compiler_params=pltpu.CompilerParams(vmem_limit_bytes=67043328),
        cost_estimate=pl.CostEstimate(
            flops=9 * count * width * pair * each,
            bytes_accessed=4 * 4 * count * width + 12 * each * chips * shard * width,
            transcendentals=count * pair * each // 2,
        ),
        name="experts",
    )(core, tokens, cot, gates, gathered, *(() if first else totals))
    return mix, rows, gate_grad.reshape(each, count).T, grads


def expert_group(tokens, cot, gates, gate_w, up_w, down_w):
    rows = tokens.shape[0]
    count, hidden = gate_w.shape[:2]
    flat = (count * hidden, D)
    gate_w, up_w, down_w = gate_w.reshape(flat), up_w.reshape(flat), down_w.reshape(flat)
    wide = jnp.broadcast_to(gates[:, :, None], (rows, count, hidden)).reshape(rows, -1)
    gate_h = lax.dot_general(tokens, gate_w, contract_last, preferred_element_type=jnp.float32)
    up_h = lax.dot_general(tokens, up_w, contract_last, preferred_element_type=jnp.float32)
    cot_h = lax.dot_general(cot, down_w, contract_last, preferred_element_type=jnp.float32)
    sigma = jax.nn.sigmoid(gate_h)
    silu = gate_h * sigma
    hidden_h = silu * up_h
    gate_grad = jnp.sum((hidden_h * cot_h).reshape(rows, count, hidden), axis=-1)
    hidden_grad = wide * cot_h
    weighted = (wide * hidden_h).astype(jnp.bfloat16)
    gate_hg = (hidden_grad * up_h * sigma * (1.0 + gate_h * (1.0 - sigma))).astype(jnp.bfloat16)
    up_hg = (hidden_grad * silu).astype(jnp.bfloat16)
    mixture = jnp.dot(weighted, down_w, preferred_element_type=jnp.float32)
    rows_grad = jnp.dot(gate_hg, gate_w, preferred_element_type=jnp.float32) + jnp.dot(
        up_hg, up_w, preferred_element_type=jnp.float32
    )
    grads = jnp.stack([
        lax.dot_general(left, right, contract_first, preferred_element_type=jnp.float32)
        .astype(jnp.bfloat16)
        .reshape(count, hidden, D)
        for left, right in ((gate_hg, tokens), (up_hg, tokens), (weighted, cot))
    ])
    return mixture, rows_grad, gate_grad, grads


def body(
    inputs,
    gain_attn,
    w_query,
    w_key,
    w_value,
    w_out,
    gain_moe,
    w_router,
    w_gate,
    w_up,
    w_down,
    routes,
    cotangent,
):
    parts = lax.axis_size("tensor")
    own_rows = inputs.shape[0]
    seq_len = own_rows * parts
    cosine, sine = rope_tables(seq_len, HD)
    inputs_f = inputs.astype(jnp.float32)
    q_cols, k_cols = w_query.shape[1], w_key.shape[1]
    proj_cols = q_cols + 2 * k_cols
    filler = jnp.zeros((w_query.shape[0], 126 - E), jnp.bfloat16)
    packed = jnp.concatenate(
        [w_query, w_key, w_value, w_out.T, w_router, gain_attn[:, None], gain_moe[:, None], filler],
        axis=1,
    )
    packed = lax.all_gather(packed, ("chip", "core"), axis=0, tiled=True)
    proj_w, out_wt, small = jnp.split(packed, [proj_cols, proj_cols + q_cols], axis=1)
    query_w, key_w, value_w = jnp.split(proj_w, [q_cols, q_cols + k_cols], axis=1)
    router_w = small[:, :E]
    gain_one_f = small[:, E].astype(jnp.float32)
    gain_two_f = small[:, E + 1].astype(jnp.float32)

    shard = w_gate.shape[1] // D
    starts = ring_chips()
    groups = GROUPS
    each = E // groups
    stacked = [w.reshape(E, shard, D) for w in (w_gate, w_up, w_down)]
    gathered = []
    for g in range(groups):
        part = jnp.stack([w[g * each : (g + 1) * each] for w in stacked])
        gathered.append(lax.all_gather(part, ("chip", "core"), axis=2, tiled=True))

    inputs_all = gather_ordered(inputs)
    inputs_all, cot_later = lax.optimization_barrier((inputs_all, cotangent))
    cot_rows = gather_rows(cot_later)
    routes_rows = sequence_routes(routes, own_rows)

    scale_one = rms_factor(inputs_f)
    inputs_all = inputs_all.astype(jnp.float32)
    normed_all = (inputs_all * rms_factor(inputs_all) * gain_one_f).astype(jnp.bfloat16)
    query_proj = jnp.dot(normed_all, query_w, preferred_element_type=jnp.float32)
    key_proj = jnp.dot(normed_all, key_w, preferred_element_type=jnp.float32)
    value_proj = jnp.dot(normed_all, value_w, preferred_element_type=jnp.float32)
    query_rot = rotate(query_proj.reshape(seq_len, -1, HD), cosine, sine).astype(jnp.bfloat16)
    key_rot = rotate(key_proj.reshape(seq_len, -1, HD), cosine, sine).astype(jnp.bfloat16)
    value_hd = value_proj.reshape(seq_len, -1, HD).astype(jnp.bfloat16)
    attn_outs, log_total = attention_forward(query_rot, key_rot, value_hd)
    attn_out = jnp.concatenate(attn_outs, axis=0)
    chunks = len(attn_outs) // 2 if parts == 2 else 1
    piece = own_rows // chunks
    hidden_parts, scale_parts, normed_parts = [], [], []
    for c in range(chunks):
        both = jnp.concatenate([attn_outs[c], attn_outs[c + chunks]], axis=0) if parts == 2 else attn_out
        hidden_part = inputs_f[c * piece : (c + 1) * piece] + scatter_tensor(
            lax.dot_general(
                both, out_wt, contract_last, preferred_element_type=jnp.float32
            ).astype(jnp.bfloat16),
            True,
        )
        scale_part = rms_factor(hidden_part)
        hidden_parts.append(hidden_part)
        scale_parts.append(scale_part)
        normed_parts.append((hidden_part * scale_part * gain_two_f).astype(jnp.bfloat16))
    hidden_mid = jnp.concatenate(hidden_parts, axis=0)
    scale_two = jnp.concatenate(scale_parts, axis=0)
    normed_two = jnp.concatenate(normed_parts, axis=0)
    if parts == 2:
        sequence = jnp.concatenate(
            normed_parts + [swap(part, "tensor") for part in normed_parts], axis=0
        )
        token_rows = jnp.concatenate([sequence, swap(sequence, "core")], axis=0)
    else:
        token_rows = gather_rows(normed_two)
    logits = jnp.dot(token_rows, router_w, preferred_element_type=jnp.float32)
    gates = dense_gates(logits, routes_rows)

    mixture, rows_grad, gate_grads, expert_sums = 0.0, 0.0, [], []
    for g in range(groups):
        token_rows_g, cot_rows_g = token_rows, cot_rows
        if g > 0:
            run_hops(expert_sums, g - 1)
            token_rows_g, cot_rows_g, mixture, rows_grad, grads, gathered[g] = tie(
                (token_rows, cot_rows, mixture, rows_grad, grads, gathered[g]),
                expert_sums,
            )
            expert_sums.append(scatter_experts(grads, g - 1, starts))
        by_core = gathered[g].reshape(3, each, -1, 2, shard, D)
        group_gates = gates[:, g * each : (g + 1) * each]
        if shard == 16 and by_core.shape[2] == 8:
            mixture, rows_grad, gate_grad, grads = expert_call(
                token_rows_g,
                cot_rows_g,
                group_gates,
                by_core,
                (mixture, rows_grad) if g > 0 else None,
            )
        else:
            by_core = lax.dynamic_index_in_dim(by_core, lax.axis_index("core"), 3, keepdims=False)
            gate_w, up_w, down_w = by_core.reshape(3, each, -1, D)
            mix, rows, gate_grad, grads = expert_group(
                token_rows_g, cot_rows_g, group_gates, gate_w, up_w, down_w
            )
            mixture, rows_grad = mixture + mix, rows_grad + rows
            grads = jnp.moveaxis(grads.reshape(3, each, -1, shard, D), 2, 0)
        gate_grads.append(gate_grad)
    run_hops(expert_sums, groups - 1)
    mixture, rows_grad, grads = tie(
        (mixture, rows_grad, grads), expert_sums
    )
    expert_sums.append(scatter_experts(grads, groups - 1, starts))
    gate_grad_own = scatter_rows(jnp.concatenate(gate_grads, axis=1))
    if parts == 2:
        probs_own = gates[:own_rows]
    else:
        probs_own = lax.dynamic_slice_in_dim(
            gates, lax.axis_index("tensor") * own_rows, own_rows, 0
        )
    logit_grad = (
        probs_own * (gate_grad_own - jnp.sum(probs_own * gate_grad_own, axis=-1, keepdims=True))
    ).astype(jnp.bfloat16)
    router_part = lax.dot_general(
        logit_grad, router_w, contract_last, preferred_element_type=jnp.float32
    )
    router_grad = lax.dot_general(
        normed_two,
        jnp.pad(logit_grad, ((0, 0), (0, 128 - E))),
        contract_first,
        preferred_element_type=jnp.float32,
    )
    half_rows = seq_len
    theirs = rows_grad[half_rows:].astype(jnp.bfloat16)
    mine = rows_grad[:half_rows] + swap(theirs, "core").astype(jnp.float32)
    mid_parts, gain_two_grad = [], 0.0
    for c in range(chunks):
        part = slice(c * piece, (c + 1) * piece)
        if parts == 2:
            given = mine[own_rows + c * piece : own_rows + (c + 1) * piece]
            summed = mine[part] + swap(given.astype(jnp.bfloat16), "tensor").astype(jnp.float32)
        else:
            summed = scatter_tensor(mine.astype(jnp.bfloat16), False)
        mid_part, gain_part = norm_backward(
            hidden_mid[part], scale_two[part], gain_two_f, summed + router_part[part]
        )
        mid_parts.append(cotangent[part].astype(jnp.float32) + mid_part)
        gain_two_grad = gain_two_grad + gain_part
    mid_grad = jnp.concatenate(mid_parts, axis=0)
    if parts == 2:
        own_low = [part.astype(jnp.bfloat16) for part in mid_parts]
        other = jnp.concatenate([swap(part, "tensor") for part in own_low], axis=0)
        own_low = jnp.concatenate(own_low, axis=0)
        first = lax.axis_index("tensor") == 0
        mid_all = jnp.concatenate(
            [jnp.where(first, own_low, other), jnp.where(first, other, own_low)], axis=0
        )
    else:
        mid_all = gather_ordered(mid_grad.astype(jnp.bfloat16))
    run_hops(expert_sums, groups)
    run_hops(expert_sums, groups + 1)
    crossing = [which for which, _ in HOPS[groups + 1]]
    mid_all, mixture = tie(
        (mid_all, mixture), [ring for k, ring in enumerate(expert_sums) if k not in crossing]
    )
    mixed = swap(mixture[seq_len:].astype(jnp.bfloat16), "core")
    mixed = (mixture[:seq_len] + mixed.astype(jnp.float32)).astype(jnp.bfloat16)
    mixed = scatter_tensor(mixed, False)
    outputs = (hidden_mid + mixed).astype(jnp.bfloat16)
    out_wt_grad = lax.dot_general(
        mid_all, attn_out, contract_first, preferred_element_type=jnp.float32
    )
    column = jnp.arange(128, dtype=jnp.int32)[None, :]
    early = jnp.concatenate(
        [
            out_wt_grad.astype(jnp.bfloat16),
            jnp.where(column == E + 1, gain_two_grad[:, None], router_grad).astype(jnp.bfloat16),
        ],
        axis=1,
    )
    early = lax.psum_scatter(early, ("chip", "core"), scatter_dimension=0, tiled=True).astype(
        jnp.float32
    )
    attn_out_grad = jnp.dot(mid_all, out_wt, preferred_element_type=jnp.float32).astype(
        jnp.bfloat16
    )
    query_grad, key_grad, value_grad = attention_backward(
        query_rot, key_rot, value_hd, log_total, attn_out_grad
    )
    run_hops(expert_sums, groups + 2)
    query_grad, key_grad, value_grad = tie((query_grad, key_grad, value_grad), expert_sums)
    query_pg = unrotate(query_grad, cosine, sine).reshape(seq_len, -1).astype(jnp.bfloat16)
    key_pg = unrotate(key_grad, cosine, sine).reshape(seq_len, -1).astype(jnp.bfloat16)
    value_pg = value_grad.reshape(seq_len, -1).astype(jnp.bfloat16)
    proj_pg = jnp.concatenate([query_pg, key_pg, value_pg], axis=1)
    proj_w_grad = lax.dot_general(
        normed_all, proj_pg, contract_first, preferred_element_type=jnp.float32
    )
    summed = lax.dot_general(
        proj_pg, proj_w, contract_last, preferred_element_type=jnp.float32
    ).astype(jnp.bfloat16)
    normed_one_grad = scatter_tensor(summed, True)
    input_part, gain_one_grad = norm_backward(inputs_f, scale_one, gain_one_f, normed_one_grad)
    input_grad = mid_grad + input_part
    late = jnp.concatenate(
        [
            proj_w_grad.astype(jnp.bfloat16),
            jnp.where(column == E, gain_one_grad[:, None], 0.0).astype(jnp.bfloat16),
        ],
        axis=1,
    )
    run_hops(expert_sums, groups + 3)
    late = lax.psum_scatter(late, ("chip", "core"), scatter_dimension=0, tiled=True).astype(
        jnp.float32
    )
    run_hops(expert_sums, groups + 4)
    shared = early[:, q_cols:] + late[:, proj_cols:]
    if parts == 2:
        shared = shared + swap(shared, "tensor")
    else:
        shared = lax.psum(shared, "tensor")
    pieces = [each_sum.result().reshape(3, each, shard * D) for each_sum in expert_sums]
    expert_grads = [jnp.concatenate([piece[k] for piece in pieces], axis=0) for k in range(3)]
    return (
        outputs,
        input_grad,
        shared[:, E],
        late[:, :q_cols],
        late[:, q_cols : q_cols + k_cols],
        late[:, q_cols + k_cols : proj_cols],
        early[:, :q_cols].T,
        shared[:, E + 1],
        shared[:, :E],
        expert_grads[0],
        expert_grads[1],
        expert_grads[2],
    )


def solution(mesh):
    dp, parts = mesh.devices.shape
    cores = jax.sharding.Mesh(mesh.devices.reshape(dp // 2, 2, parts), ("chip", "core", "tensor"))
    dp = ("chip", "core")
    every = ("chip", "core", "tensor")
    in_specs = (
        P(every, None),
        P(dp),
        P(dp, "tensor"),
        P(dp, "tensor"),
        P(dp, "tensor"),
        P("tensor", dp),
        P(dp),
        P(dp, None),
        P(None, every),
        P(None, every),
        P(None, every),
        P(dp, None),
        P(every, None),
    )
    out_specs = (
        P(every, None),
        P(every, None),
        P(dp),
        P(dp, "tensor"),
        P(dp, "tensor"),
        P(dp, "tensor"),
        P("tensor", dp),
        P(dp),
        P(dp, None),
        P(None, every),
        P(None, every),
        P(None, every),
    )

    return jax.shard_map(body, mesh=cores, in_specs=in_specs, out_specs=out_specs, check_vma=False)
```
